128 devices in a mesh: aa: 16 (over y, x), ba: 8 (over z, core).
Axes of the slice: x: 4, y: 4, z: 4, core: 2. Of those that a mesh axis runs over, the one named last changes fastest.
Arguments:
- queries: bfloat16 [8, 128, 8192], P('ba', None, 'aa'), may hold values from -10 to 10
- new_kv: bfloat16 [8, 128, 2, 512], P('ba', 'aa'), may hold values from -4 to 4
- pool: bfloat16 [8, 192, 32, 2, 512], P('ba', 'aa'), may hold values from -4 to 4
- page_table: int32 [8, 64], P('ba', 'aa'), may hold values from 0 to 11, as said below
- ctx_len: int32 [8, 16], P('ba', 'aa'), may hold values from 1 to 128, as said below
- move_page: int32 [8, 112], P('ba', 'aa'), may hold values from 0 to 11, as said below
- move_dest: int32 [8, 112], P('ba', 'aa'), may hold values from 0 to 7, as said below
- append_page: int32 [8, 16], P('ba', 'aa'), may hold values from 0 to 11
Outputs:
- attended: bfloat16 [8, 128, 8192], P('ba', None, 'aa')
- pool_out: bfloat16 [8, 192, 32, 2, 512], P('ba', 'aa')
The draws below stay inside these ranges and needn't reach their ends.
Inputs may be any that keep to these rules, and one draw needn't show every extreme that they name: `page_table`: the entries of one device are distinct pages of its pool and differ from its leaving pages and its append page. `ctx_len`: for each instance some index of aa holds exactly 128 live rows. `move_page`: the 7 entries of one device are distinct pages of its pool. `move_dest`: A device never names its own instance and names any one instance at most 2 times; for each index of aa one instance is named exactly 2 times by the device of every other instance.
All inputs are finite; a program needn't handle non-finite values.
Results may differ from the reference program's by a relative error of at most 0.0017.
Values may be sent and summed in bfloat16 or wider, within the bound.
No kernel may reach another device: no remote copies, remote signals or barrier semaphores. Data moves between devices by JAX's collectives and lax.ppermute only.
A program may use at most 64 MiB of HBM per device.

```python
import math
import jax
import jax.numpy as jnp
from jax import lax

HEADS = 64
KV_HEADS = 4
HEAD_DIM = 128
PAGE = 32
MOST = 2
NEW_ROWS = 128
TABLE = 4
GROUP = 16
INSTANCES = 8
MOVES = 7
POOL = 12
NEW_DEV = 8
N_AA = 16


def draw_new_kv(key, part):
    out_shape = (INSTANCES, NEW_ROWS, 2, KV_HEADS * HEAD_DIM)
    values = jnp.clip(jax.random.normal(jax.random.fold_in(key, 71), out_shape, jnp.float32), -4.0, 4.0)
    return values.astype(jnp.bfloat16)


def draw_queries(key, part):
    out_shape = (INSTANCES, NEW_ROWS, HEADS * HEAD_DIM)
    drawn = 2.5 * jax.random.normal(jax.random.fold_in(key, 75), out_shape, jnp.float32)
    return jnp.clip(drawn, -10.0, 10.0).astype(jnp.bfloat16)


def shuffle_pages(sub_key):
    return jax.random.permutation(sub_key, POOL).astype(jnp.int32)


def page_lists(key):
    sub_keys = jax.random.split(jax.random.fold_in(key, 31), INSTANCES * N_AA)
    orders = jax.vmap(shuffle_pages)(sub_keys)
    return orders.reshape(INSTANCES, N_AA, POOL)


def draw_page_table(key, part):
    return page_lists(key)[:, :, :TABLE].reshape(INSTANCES, N_AA * TABLE)


def draw_move_page(key, part):
    return page_lists(key)[:, :, TABLE:TABLE + MOVES].reshape(INSTANCES, N_AA * MOVES)


def draw_append_page(key, part):
    return page_lists(key)[:, :, TABLE + MOVES]


def shuffle_slots(sub_key):
    return jax.random.permutation(sub_key, (INSTANCES - 1) * MOST).astype(jnp.int32)


def draw_move_dest(key, part):
    seeded = jax.random.fold_in(key, 37)
    option_count = (INSTANCES - 1) * MOST
    busiest = jax.random.randint(jax.random.fold_in(seeded, 1), (N_AA,), 0, INSTANCES)
    source = jnp.arange(INSTANCES)[:, None]
    candidate = (source + 1 + jnp.arange(option_count)[None, :] // MOST) % INSTANCES
    sub_keys = jax.random.split(jax.random.fold_in(seeded, 2), INSTANCES * N_AA)
    scores = jax.vmap(shuffle_slots)(sub_keys).reshape(INSTANCES, N_AA, option_count)
    forced = candidate[:, None, :] == busiest[None, :, None]
    priority = jnp.where(forced, scores + option_count, scores)
    picked = lax.top_k(priority, MOVES)[1]
    spread = jnp.broadcast_to(candidate[:, None, :], priority.shape)
    chosen_dest = jnp.take_along_axis(spread, picked, axis=-1)
    return chosen_dest.reshape(INSTANCES, N_AA * MOVES).astype(jnp.int32)


def draw_ctx_len(key, part):
    seeded = jax.random.fold_in(key, 41)
    full_rows = TABLE * PAGE
    lengths = jax.random.randint(jax.random.fold_in(seeded, 1), (INSTANCES, N_AA), 1, full_rows + 1)
    full_index = jax.random.randint(jax.random.fold_in(seeded, 2), (INSTANCES,), 0, N_AA)
    hit_full = jnp.arange(N_AA)[None, :] == full_index[:, None]
    return jnp.where(hit_full, full_rows, lengths).astype(jnp.int32)


def shard_levels(own_key, dims, shards, smallest, top_value):
    level = 1.0
    for dim, parts in shards:
        steps = jax.random.uniform(jax.random.fold_in(jax.random.fold_in(own_key, 6), dim), (parts,), jnp.float32, smallest / len(shards), top_value / len(shards))
        level = level * jnp.repeat(jnp.exp(steps), dims[dim] // parts).reshape((-1,) + (1,) * (len(dims) - 1 - dim))
    return level


def scatter_about(key, shape, scale, most, cuts=(), kind=jnp.bfloat16):
    level = shard_levels(key, shape, cuts, -0.22, 0.18) if cuts else 1.0
    values = jax.random.normal(key, shape, jnp.float32) * scale * level
    return jnp.minimum(jnp.maximum(values, -most), most).astype(kind)


def setup_inputs(seed: int = 0) -> dict:
    key_list = jax.random.split(jax.random.key(seed), 9)
    queries = draw_queries(jax.random.fold_in(key_list[8], 71), 0)
    new_kv = draw_new_kv(jax.random.fold_in(key_list[8], 71), 0)
    pool = scatter_about(key_list[2], (INSTANCES, N_AA * POOL, PAGE, 2, KV_HEADS * HEAD_DIM), 1.0, 4.0, ((0, 8), (1, 16)))
    page_table = draw_page_table(jax.random.fold_in(key_list[8], 71), 0)
    ctx_len = draw_ctx_len(jax.random.fold_in(key_list[8], 71), 0)
    move_page = draw_move_page(jax.random.fold_in(key_list[8], 71), 0)
    move_dest = draw_move_dest(jax.random.fold_in(key_list[8], 71), 0)
    append_page = draw_append_page(jax.random.fold_in(key_list[8], 71), 0)
    return dict(queries=queries, new_kv=new_kv, pool=pool, page_table=page_table, ctx_len=ctx_len, move_page=move_page, move_dest=move_dest, append_page=append_page)


def pick_pages(pages, page_ids):
    return jnp.take(pages, page_ids.astype(jnp.int32), axis=0)

def place_rows(pages, fresh_rows, page_id):
    start = page_id.astype(jnp.int32)
    zero = jnp.zeros((), jnp.int32)
    return lax.dynamic_update_slice(pages, fresh_rows[None], (start, zero, zero, zero))

def attention(query_rows, key_rows, visible):
    query_heads = query_rows.astype(jnp.float32).reshape(NEW_ROWS, KV_HEADS, GROUP, HEAD_DIM).transpose(1, 0, 2, 3)
    head_keys = key_rows[:, 0].astype(jnp.float32).reshape(-1, KV_HEADS, HEAD_DIM).transpose(1, 0, 2)
    head_values = key_rows[:, 1].astype(jnp.float32).reshape(-1, KV_HEADS, HEAD_DIM).transpose(1, 0, 2)

    def one_head(operands):
        head_query, key_block, value_block = operands
        scores = jnp.einsum('qgd,rd->qgr', head_query, key_block) / math.sqrt(HEAD_DIM)
        scores = jnp.where(visible[:, None, :], scores, -jnp.inf)
        row_top = lax.optimization_barrier(jnp.max(scores, axis=-1, keepdims=True))
        weights = jnp.exp(scores - row_top)
        row_total = lax.optimization_barrier(jnp.sum(weights, axis=-1))
        return jnp.einsum('qgr,rd->qgd', weights, value_block, precision=lax.Precision.HIGHEST) / row_total[..., None]
    outputs = lax.map(one_head, (query_heads, head_keys, head_values))
    return outputs.transpose(1, 0, 2, 3).reshape(NEW_ROWS, HEADS * HEAD_DIM).astype(jnp.bfloat16)

def reference(queries, new_kv, pool, page_table, ctx_len, move_page, move_dest, append_page):
    kv_width = KV_HEADS * HEAD_DIM
    pool_pages = pool.reshape(INSTANCES, N_AA, POOL, PAGE, 2, kv_width)
    tables = page_table.reshape(INSTANCES, N_AA, TABLE)
    moved_ids = move_page.reshape(INSTANCES, N_AA, MOVES)
    targets = move_dest.reshape(INSTANCES, N_AA, MOVES)
    counter = jnp.arange(MOVES, dtype=jnp.int32)
    earlier = counter[None, :] < counter[:, None]
    same_target = targets[..., :, None] == targets[..., None, :]
    ranks = lax.optimization_barrier(jnp.sum(same_target & earlier, axis=-1)).astype(jnp.int32)
    pick_all = jax.vmap(jax.vmap(pick_pages))
    slot_numbers = jnp.arange(MOST, dtype=jnp.int32)
    row_offsets = jnp.arange(TABLE * PAGE, dtype=jnp.int32)
    causal = jnp.arange(NEW_ROWS, dtype=jnp.int32)[None, :] <= jnp.arange(NEW_ROWS, dtype=jnp.int32)[:, None]

    def serve_instance(target):
        slot_hit = (targets == target)[..., None] & (ranks[..., None] == slot_numbers)
        page_ids = lax.optimization_barrier(jnp.sum(jnp.where(slot_hit, moved_ids[..., None], 0), axis=2)).astype(jnp.int32)
        arrived = jnp.any(slot_hit, axis=2)
        moved_rows = pick_all(pool_pages, page_ids).reshape(-1, 2, kv_width)
        moved_live = jnp.broadcast_to(arrived[..., None], (INSTANCES, N_AA, MOST, PAGE)).reshape(-1)
        own_pages = lax.dynamic_index_in_dim(pool_pages, target, 0, keepdims=False)
        own_table = lax.dynamic_index_in_dim(tables, target, 0, keepdims=False)
        own_rows = jax.vmap(pick_pages)(own_pages, own_table).reshape(-1, 2, kv_width)
        lengths = lax.dynamic_index_in_dim(ctx_len, target, 0, keepdims=False)
        own_live = (row_offsets[None, :] < lengths[:, None]).reshape(-1)
        fresh_rows = lax.dynamic_index_in_dim(new_kv, target, 0, keepdims=False)
        key_rows = jnp.concatenate([own_rows, moved_rows, fresh_rows], axis=0)
        visible = jnp.concatenate([jnp.broadcast_to(own_live[None, :], (NEW_ROWS, own_live.shape[0])), jnp.broadcast_to(moved_live[None, :], (NEW_ROWS, moved_live.shape[0])), causal], axis=1)
        query_rows = lax.dynamic_index_in_dim(queries, target, 0, keepdims=False)
        return attention(query_rows, key_rows, visible)
    attended = lax.map(serve_instance, jnp.arange(INSTANCES, dtype=jnp.int32))
    fresh_all = new_kv.reshape(INSTANCES, N_AA, NEW_DEV, 2, kv_width)
    updated = jax.vmap(jax.vmap(place_rows))(pool_pages, fresh_all, append_page)
    return (attended, updated.reshape(pool.shape))
```

```python
import functools
import math

import jax
import jax.numpy as jnp
import numpy as np
from jax import lax
from jax.experimental import pallas as pl
from jax.experimental.pallas import tpu as pltpu
from jax.sharding import Mesh, PartitionSpec as P

D = 128
KVH = 4
MOST = 2
PAGE = 32
TABLE = 4
MOVES = 7
INST = 8
NEW_DEV = 8
NQ = 128
RES = TABLE * PAGE + NEW_DEV
DEAD = 128.0
BIG = -1e30
BF = jnp.bfloat16
F32 = jnp.float32
LOG_SCALE = math.log2(math.e) / math.sqrt(D)
MIG_BLOCKS = INST * KVH * MOST * PAGE // 128
RES_BLOCKS = TABLE * PAGE * KVH // 128
BLOCKS = MIG_BLOCKS + RES_BLOCKS + 1
ROWS = BLOCKS * 128


def pack_kernel(table, ctx, page, dest, pool, new, mig, res, dead, sem_m, sem_r):
    dead[...] = jnp.full_like(dead, DEAD)
    for y in range(KVH):
        lanes = pl.ds(y * D, D)
        for j in range(TABLE):
            pltpu.make_async_copy(
                pool.at[table[0, j], :, :, lanes], res.at[y, pl.ds(j * PAGE, PAGE)], sem_r
            ).start()
        pltpu.make_async_copy(
            new.at[:, :, lanes], res.at[y, pl.ds(TABLE * PAGE, NEW_DEV)], sem_r
        ).start()
    for m in range(MOVES):
        rank = jnp.int32(0)
        for e in range(m):
            rank += (dest[0, e] == dest[0, m]).astype(jnp.int32)
        for y in range(KVH):
            pltpu.make_async_copy(
                pool.at[page[0, m], :, :, pl.ds(y * D, D)], mig.at[dest[0, m], y, rank], sem_m
            ).start()
    for d in range(INST):
        count = jnp.int32(0)
        for m in range(MOVES):
            count += (dest[0, m] == d).astype(jnp.int32)
        for s in range(MOST):

            @pl.when(count <= s)
            def _():
                pltpu.make_async_copy(dead, mig.at[d, :, s], sem_m).start()

    pltpu.make_async_copy(res, res, sem_r).wait()
    index = lax.broadcasted_iota(jnp.int32, (TABLE * PAGE, 2, D), 0)
    alive = index < ctx[0, 0]
    for y in range(KVH):
        part = res[y, : TABLE * PAGE].astype(F32)
        res[y, : TABLE * PAGE] = jnp.where(alive, part, DEAD).astype(BF)
    pltpu.make_async_copy(mig, mig, sem_m).wait()


def pack(table, ctx, page, dest, pool, new):
    smem = pl.BlockSpec(memory_space=pltpu.SMEM)
    hbm = pl.BlockSpec(memory_space=pl.ANY)
    vmem = pl.BlockSpec(memory_space=pltpu.VMEM)
    return pl.pallas_call(
        pack_kernel,
        in_specs=[smem] * 4 + [hbm] * 2,
        out_specs=[hbm, vmem],
        out_shape=[
            jax.ShapeDtypeStruct((INST, KVH, MOST, PAGE, 2, D), BF),
            jax.ShapeDtypeStruct((KVH, RES, 2, D), BF),
        ],
        scratch_shapes=[
            pltpu.VMEM((KVH, PAGE, 2, D), BF),
            pltpu.SemaphoreType.DMA,
            pltpu.SemaphoreType.DMA,
        ],
        compiler_params=pltpu.CompilerParams(vmem_limit_bytes=16 << 20),
    )(table, ctx, page, dest, pool, new)


def attend_kernel(
    place, q0, q1, q2, q3, mig, res, new, o_ref, n_ref, d_ref, kt, vv, sc, aug
):
    row = lax.broadcasted_iota(jnp.int32, (256, 256), 0)
    col = lax.broadcasted_iota(jnp.int32, (256, 256), 1)
    pick = (row == jnp.where(col < 128, 2 * col, 2 * col - 255)).astype(BF)
    sub = lax.broadcasted_iota(jnp.int32, (128, 128), 0)
    lane = lax.broadcasted_iota(jnp.int32, (128, 128), 1)

    def put(b, x):
        both = lax.dot_general(x, pick, (((0,), (0,)), ((), ())), preferred_element_type=F32)
        keys = both[:, :128]
        cols = pl.ds(pl.multiple_of(b * 128, 128), 128)
        kt[0:128, cols] = keys.astype(BF)
        kt[128:256, cols] = jnp.where((sub == 0) & (keys > 64.0), BIG, 0.0).astype(BF)
        vals = lax.dot_general(
            pick[:, 128:], x, (((0,), (0,)), ((), ())), preferred_element_type=F32
        )
        rows = pl.ds(pl.multiple_of(b * 128, 128), 128)
        vv[rows, 0:128] = vals.astype(BF)
        vv[rows, 128:256] = jnp.ones((128, 128), BF)

    def mig_step(b, c):
        put(b, mig[b])
        return c

    lax.fori_loop(0, MIG_BLOCKS, mig_step, 0)

    def res_step(b, c):
        put(MIG_BLOCKS + b, res[b])
        return c

    lax.fori_loop(0, RES_BLOCKS, res_step, 0)
    last = BLOCKS - 1
    put(last, jnp.concatenate([new[...], jnp.zeros((192, 128), BF)], axis=0))
    hot = jnp.where((sub == 1 + lane) & (lane < 32), 1.0, 0.0)
    kt[128:256, last * 128 :] = jnp.where((sub == 0) & (lane >= 32), BIG, hot).astype(BF)
    j = lane - 1
    pos = (j // 8) * 32 + place[0] * 8 + j % 8
    bar = jnp.where((lane >= 1) & (lane < 33) & (pos > sub), BIG, 0.0)
    aug[...] = jnp.where(lane == 0, 1.0, bar).astype(BF)

    qs = (q0, q1, q2, q3)
    for k in range(4):
        num = jnp.zeros((128, 128), F32)
        den = jnp.zeros((128, 128), F32)
        for h in range(4):
            lanes = slice(h * D, h * D + D)
            q = jnp.concatenate([qs[k][:, lanes], aug[...]], axis=1)
            s = jnp.dot(q, kt[...], preferred_element_type=F32)
            top = jnp.max(s, axis=1, keepdims=True)
            p = jnp.exp2((s - top) * LOG_SCALE)
            high = p.astype(BF)
            low = (p - high.astype(F32)).astype(BF)
            o = jnp.dot(high, vv[...], preferred_element_type=F32)
            o += jnp.dot(low, vv[...], preferred_element_type=F32)
            total = o[:, 128:]
            mean = o[:, :128] / total
            most = jnp.maximum(jnp.max(jnp.abs(mean), axis=1, keepdims=True), 1e-30)
            o_ref[k, :, lanes] = mean / most
            lse = jnp.log2(total) + top * LOG_SCALE
            den = jnp.where(lane == h, lse, den)
            num = jnp.where(lane == h, lse + jnp.log2(most), num)
        n_ref[k] = num
        d_ref[k] = den


def attend(place, qs, mig, res, new):
    vmem = pl.BlockSpec(memory_space=pltpu.VMEM)
    return pl.pallas_call(
        attend_kernel,
        in_specs=[pl.BlockSpec(memory_space=pltpu.SMEM)] + [vmem] * 7,
        out_specs=[vmem] * 3,
        out_shape=[
            jax.ShapeDtypeStruct((4, 128, 512), F32),
            jax.ShapeDtypeStruct((4, 128, 128), F32),
            jax.ShapeDtypeStruct((4, 128, 128), F32),
        ],
        scratch_shapes=[
            pltpu.VMEM((256, ROWS), BF),
            pltpu.VMEM((ROWS, 256), BF),
            pltpu.VMEM((128, ROWS), F32),
            pltpu.VMEM((128, 128), BF),
        ],
        compiler_params=pltpu.CompilerParams(vmem_limit_bytes=56 << 20),
    )(place, *qs, mig, res, new)


def local(queries, new_kv, pool, page_table, ctx_len, move_page, move_dest, append_page):
    pool_pages = pool[0]
    fresh = new_kv[0]
    q = queries[0]
    mig, res = pack(page_table, ctx_len, move_page, move_dest, pool_pages, fresh)
    mig = mig.reshape(INST * KVH, MOST * PAGE * 2, D)
    mig = lax.all_to_all(mig, ("ba", "y"), 0, 0, tiled=True)
    res = lax.all_to_all(res.reshape(KVH, RES * 2, D), "y", 0, 0, tiled=True)
    qs = [q] + [
        lax.ppermute(q, "x", [(i, (i + k) % 4) for i in range(4)]) for k in range(1, 4)
    ]
    old = res[:, : TABLE * PAGE * 2].reshape(RES_BLOCKS, 256, D)
    new = res[:, TABLE * PAGE * 2 :].reshape(KVH * NEW_DEV * 2, D)
    place = lax.axis_index("x").astype(jnp.int32).reshape(1)
    out, num, den = attend(place, qs, mig.reshape(MIG_BLOCKS, 256, D), old, new)
    outs, nums, dens = [out[0]], [num[0, :, :4]], [den[0, :, :4]]
    for k in range(1, 4):
        stats = jnp.concatenate([num[k, :, :4], den[k, :, :4]], axis=1)
        high = lax.reduce_precision(stats, 5, 10)
        low = (stats - high).astype(jnp.float16)
        high = high.astype(jnp.float16)
        extra = jnp.concatenate([high, low], axis=1).reshape(4, 512)
        sent = jnp.concatenate([out[k].astype(jnp.float16), extra], axis=0)
        got = lax.ppermute(sent, "x", [(i, (i - k) % 4) for i in range(4)])
        extra = got[128:].reshape(128, 16).astype(F32)
        stats = extra[:, :8] + extra[:, 8:]
        outs.append(got[:128].astype(F32))
        nums.append(stats[:, :4])
        dens.append(stats[:, 4:])
    top = functools.reduce(jnp.maximum, dens)
    total = sum(jnp.exp2(x - top) for x in dens)
    result = sum(
        o.reshape(128, 4, D) * (jnp.exp2(n - top) / total)[:, :, None] for o, n in zip(outs, nums)
    )
    attended = result.reshape(1, NQ, 4 * D).astype(BF)
    zero = jnp.zeros((), jnp.int32)
    updated = lax.dynamic_update_slice(
        pool_pages, fresh[None], (append_page[0, 0], zero, zero, zero)
    )
    return attended, updated[None]


def solution(mesh):
    grid = Mesh(np.asarray(mesh.devices).reshape(4, 4, 8), ("y", "x", "ba"))
    aa = ("y", "x")
    return jax.shard_map(
        local,
        mesh=grid,
        in_specs=(
            P("ba", None, aa),
            P("ba", aa, None, None),
            P("ba", aa, None, None, None),
            P("ba", aa),
            P("ba", aa),
            P("ba", aa),
            P("ba", aa),
            P("ba", aa),
        ),
        out_specs=(P("ba", None, aa), P("ba", aa, None, None, None)),
        check_vma=False,
    )
```

```python
import functools
import math

import jax
import jax.numpy as jnp
import numpy as np
from jax import lax
from jax.experimental import pallas as pl
from jax.experimental.pallas import tpu as pltpu
from jax.sharding import Mesh, PartitionSpec as P

D = 128
KVH = 4
MOST = 2
PAGE = 32
TABLE = 4
MOVES = 7
INST = 8
NEW_DEV = 8
NQ = 128
RES = TABLE * PAGE + NEW_DEV
DEAD = 128.0
BIG = -1e30
BF = jnp.bfloat16
F32 = jnp.float32
F16 = jnp.float16
LOG_SCALE = math.log2(math.e) / math.sqrt(D)
HALF = MOST * PAGE
REST = RES - HALF
MIG_ROWS = INST * KVH * MOST * PAGE
OLD_ROWS = (TABLE - MOST) * PAGE * KVH
ROWS = MIG_ROWS + OLD_ROWS + 128
CHUNK = 256

SMEM = pl.BlockSpec(memory_space=pltpu.SMEM)
HBM = pl.BlockSpec(memory_space=pltpu.HBM)
VMEM = pl.BlockSpec(memory_space=pltpu.VMEM)


def here():
    return (
        lax.axis_index("x").astype(jnp.int32),
        lax.axis_index("y").astype(jnp.int32),
        lax.axis_index("ba").astype(jnp.int32),
    )


def pack_kernel(
    table_in, ctx_in, page_in, dest_in, source, new, mig, r0, r1, r2, r3, table, ctx, page, dest,
    pool, dead, sem_s, sem_p, sem_m, sem_r
):
    fetch = pltpu.make_async_copy(source, pool, sem_p)
    fetch.start()
    scalars = [
        pltpu.make_async_copy(a, b, sem_s.at[i])
        for i, (a, b) in enumerate(
            ((table_in, table), (ctx_in, ctx), (page_in, page), (dest_in, dest))
        )
    ]
    for copy in scalars:
        copy.start()
    dead[...] = jnp.full_like(dead, DEAD)
    _, y_here, b_here = here()
    for copy in scalars:
        copy.wait()
    for d in range(INST):
        count = jnp.int32(0)
        for m in range(MOVES):
            count += (dest[0, m] == d).astype(jnp.int32)
        for s in range(MOST):

            @pl.when((count <= s) & (b_here != d))
            def _():
                pltpu.make_async_copy(dead, mig.at[d, :, s], sem_m).start()

    fetch.wait()
    for m in range(MOVES):
        rank = jnp.int32(0)
        for e in range(m):
            rank += (dest[0, e] == dest[0, m]).astype(jnp.int32)
        for y in range(KVH):
            pltpu.make_async_copy(
                pool.at[page[0, m], :, :, pl.ds(y * D, D)], mig.at[dest[0, m], y, rank], sem_m
            ).start()
    index = lax.broadcasted_iota(jnp.int32, (PAGE, 2, KVH * D), 0)
    for j in range(TABLE):
        page_j = table[0, j]

        @pl.when(ctx[0, 0] < (j + 1) * PAGE)
        def _():
            rows = pool[page_j].astype(F32)
            alive = index < ctx[0, 0] - j * PAGE
            pool[page_j] = jnp.where(alive, rows, DEAD).astype(BF)

    outs = (r0, r1, r2, r3)
    for k in range(4):
        lanes = pl.ds(pl.multiple_of(lax.rem(y_here + k, 4) * D, D), D)
        for j in range(MOST, TABLE):
            pltpu.make_async_copy(
                pool.at[table[0, j], :, :, lanes],
                outs[k].at[pl.ds((j - MOST) * PAGE, PAGE)],
                sem_r.at[k],
            ).start()
        pltpu.make_async_copy(
            new.at[:, :, lanes], outs[k].at[pl.ds((TABLE - MOST) * PAGE, NEW_DEV)], sem_r.at[k]
        ).start()
    for j in range(MOST):
        for y in range(KVH):
            pltpu.make_async_copy(
                pool.at[table[0, j], :, :, pl.ds(y * D, D)], mig.at[b_here, y, j], sem_m
            ).start()
    for k in range(4):
        pltpu.make_async_copy(outs[k], outs[k], sem_r.at[k]).wait()
    pltpu.make_async_copy(mig, mig, sem_m).wait()


def pack(table, ctx, page, dest, pool, new):
    return pl.pallas_call(
        pack_kernel,
        in_specs=[HBM] * 5 + [VMEM],
        out_specs=[HBM] * 5,
        out_shape=[jax.ShapeDtypeStruct((INST, KVH, MOST, PAGE, 2, D), BF)]
        + [jax.ShapeDtypeStruct((REST, 2, D), BF)] * 4,
        scratch_shapes=[pltpu.SMEM(a.shape, jnp.int32) for a in (table, ctx, page, dest)]
        + [
            pltpu.VMEM(pool.shape, BF),
            pltpu.VMEM((KVH, PAGE, 2, D), BF),
            pltpu.SemaphoreType.DMA((4,)),
            pltpu.SemaphoreType.DMA,
            pltpu.SemaphoreType.DMA,
            pltpu.SemaphoreType.DMA((4,)),
        ],
        compiler_params=pltpu.CompilerParams(vmem_limit_bytes=60 << 20),
        name="pack",
    )(table, ctx, page, dest, pool, new)


def append_kernel(page_in, after, source, new, target, page, pool, sem):
    copy = pltpu.make_async_copy(source, pool, sem.at[0])
    copy.start()
    scalar = pltpu.make_async_copy(page_in, page, sem.at[1])
    scalar.start()
    scalar.wait()
    copy.wait()
    last = pltpu.make_async_copy(new, pool.at[page[0, 0], pl.ds(0, NEW_DEV)], sem.at[1])
    last.start()
    last.wait()
    copy = pltpu.make_async_copy(pool, target, sem.at[0])
    copy.start()
    copy.wait()


def append(page, after, pool, new):
    return pl.pallas_call(
        append_kernel,
        in_specs=[HBM] * 4,
        out_specs=HBM,
        out_shape=jax.ShapeDtypeStruct(pool.shape, BF),
        scratch_shapes=[
            pltpu.SMEM((1, 1), jnp.int32),
            pltpu.VMEM(pool.shape, BF),
            pltpu.SemaphoreType.DMA((2,)),
        ],
        compiler_params=pltpu.CompilerParams(vmem_limit_bytes=8 << 20),
        name="append",
    )(page, after, pool, new)


def pickers():
    row = lax.broadcasted_iota(jnp.int32, (256, 128), 0)
    col = lax.broadcasted_iota(jnp.int32, (256, 128), 1)
    keys = (row == 2 * col).astype(BF)
    row = lax.broadcasted_iota(jnp.int32, (128, 256), 0)
    col = lax.broadcasted_iota(jnp.int32, (128, 256), 1)
    return keys, (col == 2 * row + 1).astype(BF)


def put(x, pick, kt, vv, at):
    keys = lax.dot_general(x, pick[0], (((0,), (0,)), ((), ())), preferred_element_type=F32)
    kt[0:128, at] = keys.astype(BF)
    sub = lax.broadcasted_iota(jnp.int32, (128, 128), 0)
    kt[128:256, at] = jnp.where((sub == 0) & (keys > 64.0), BIG, 0.0).astype(BF)
    vals = jnp.dot(pick[1], x, preferred_element_type=F32)
    vv[at, 0:128] = vals.astype(BF)
    vv[at, 128:256] = jnp.ones((128, 128), BF)


def fill(mig, parts, kt, vv, aug):
    x_here, y_here, _ = here()
    pick = pickers()
    for i in range(MIG_ROWS // 128):
        put(mig[i], pick, kt, vv, slice(i * 128, i * 128 + 128))
    for i in range(2):
        x = jnp.concatenate([parts[2 * i][0:128], parts[2 * i + 1][0:128]], axis=0)
        at = MIG_ROWS + i * 128
        put(x, pick, kt, vv, slice(at, at + 128))
    at = MIG_ROWS + OLD_ROWS
    fresh = [r[128:144] for r in parts] + [jnp.zeros((192, 128), BF)]
    put(jnp.concatenate(fresh, axis=0), pick, kt, vv, slice(at, at + 128))
    sub = lax.broadcasted_iota(jnp.int32, (128, 128), 0)
    lane = lax.broadcasted_iota(jnp.int32, (128, 128), 1)
    hot = jnp.where((sub == 1 + lane) & (lane < 32), 1.0, 0.0)
    kt[128:256, at : at + 128] = jnp.where((sub == 0) & (lane >= 32), BIG, hot).astype(BF)
    j = lane - 1
    source = (y_here + 4 - (j >> 3)) & 3
    pos = source * 32 + x_here * 8 + (j & 7)
    bar = jnp.where((lane >= 1) & (lane < 33) & (pos > sub), BIG, 0.0)
    aug[...] = jnp.where(lane == 0, 1.0, bar).astype(BF)


def rows_of(qs, outs, kt, vv, aug, s_ref):
    per = CHUNK // 128
    units = [(i, c) for i in range(len(qs)) for c in range(512 // CHUNK)]
    lane = lax.broadcasted_iota(jnp.int32, (128, 128), 1)
    stats = [jnp.zeros((128, 128), F32) for _ in qs]

    def score(u):
        i, c = units[u]
        q = [
            jnp.concatenate([qs[i][:, (c * per + h) * 128 : (c * per + h + 1) * 128], aug[...]], 1)
            for h in range(per)
        ]
        s_ref[u % 2] = jnp.dot(jnp.concatenate(q, 0), kt[...], preferred_element_type=F32)

    score(0)
    for u, (i, c) in enumerate(units):
        if u + 1 < len(units):
            score(u + 1)
        s = s_ref[u % 2]
        top = jnp.max(s, axis=1, keepdims=True)
        p = jnp.exp2((s - top) * LOG_SCALE)
        high = p.astype(BF)
        low = (p - high.astype(F32)).astype(BF)
        o = jnp.dot(high, vv[...], preferred_element_type=F32)
        o += jnp.dot(low, vv[...], preferred_element_type=F32)
        total = o[:, 128:]
        mean = o[:, :128] / total
        most = jnp.maximum(jnp.max(jnp.abs(mean), axis=1, keepdims=True), 1e-30)
        mean = mean / most
        lse = jnp.log2(total) + top * LOG_SCALE
        num = lse + jnp.log2(most)
        for h in range(per):
            part = slice(h * 128, h * 128 + 128)
            at = c * per + h
            outs[i][0:128, at * 128 : at * 128 + 128] = mean[part]
            stats[i] = jnp.where(lane == at, lse[part], stats[i])
            stats[i] = jnp.where(lane == 4 + at, num[part], stats[i])
    for i, out in enumerate(outs):
        rows = stats[i].T[0:8]
        high = jnp.floor(rows * 2.0 + 0.5) * 0.5
        out[128:136, 0:128] = high
        out[128:136, 128:256] = rows - high
        out[128:136, 256:512] = jnp.zeros((8, 256), F32)


def first_kernel(q, mig, r0, r1, r2, r3, out, kt, vv, aug, s_ref):
    fill(mig, (r0, r1, r2, r3), kt, vv, aug)
    rows_of((q,), (out,), kt, vv, aug, s_ref)


def more_kernel(*refs):
    *pairs, kt, vv, aug = refs[: len(refs) // 2 + 1]
    outs = refs[len(refs) // 2 + 1 : -1]
    rows_of(pairs, outs, kt, vv, aug, refs[-1])


def cost(count):
    return pl.CostEstimate(
        flops=3 * 2 * 512 * ROWS * 256 * count,
        transcendentals=512 * ROWS * count,
        bytes_accessed=(2 << 20) * count,
    )


PART = jax.ShapeDtypeStruct((136, 512), F32)
SCORES = pltpu.VMEM((2, CHUNK, ROWS), F32)


def first(q, mig, parts):
    return pl.pallas_call(
        first_kernel,
        in_specs=[VMEM] * 6,
        out_specs=[VMEM] * 4,
        out_shape=[
            PART,
            jax.ShapeDtypeStruct((256, ROWS), BF),
            jax.ShapeDtypeStruct((ROWS, 256), BF),
            jax.ShapeDtypeStruct((128, 128), BF),
        ],
        scratch_shapes=[SCORES],
        compiler_params=pltpu.CompilerParams(vmem_limit_bytes=28 << 20),
        cost_estimate=cost(1),
        name="first",
    )(q, mig, *parts)


def more(qs, kt, vv, aug):
    return pl.pallas_call(
        more_kernel,
        in_specs=[VMEM] * (len(qs) + 3),
        out_specs=[VMEM] * len(qs),
        out_shape=[PART] * len(qs),
        scratch_shapes=[SCORES],
        compiler_params=pltpu.CompilerParams(vmem_limit_bytes=28 << 20),
        cost_estimate=cost(len(qs)),
        name="more",
    )(*qs, kt, vv, aug)


def combine_kernel(g0, g1, g2, g3, out):
    parts = (g0, g1, g2, g3)
    stats = [g[128:136, 0:128] + g[128:136, 128:256] for g in parts]
    cols = jnp.concatenate(stats + [jnp.zeros((96, 128), F32)], axis=0).T
    for h in range(4):
        dens = [cols[:, 8 * k + h : 8 * k + h + 1] for k in range(4)]
        nums = [cols[:, 8 * k + 4 + h : 8 * k + 5 + h] for k in range(4)]
        top = functools.reduce(jnp.maximum, dens)
        total = sum(jnp.exp2(x - top) for x in dens)
        lanes = slice(h * 128, h * 128 + 128)
        result = sum(g[0:128, lanes] * (jnp.exp2(n - top) / total) for g, n in zip(parts, nums))
        out[:, lanes] = result.astype(BF)


def combine(parts):
    return pl.pallas_call(
        combine_kernel,
        in_specs=[VMEM] * 4,
        out_specs=VMEM,
        out_shape=jax.ShapeDtypeStruct((128, 512), BF),
        compiler_params=pltpu.CompilerParams(vmem_limit_bytes=8 << 20),
        name="combine",
    )(*parts)


def shift(value, axis, k):
    return lax.ppermute(value, axis, [(i, (i + k) % 4) for i in range(4)])


def back(out, k):
    return shift(out.astype(F16), "x", -k).astype(F32)


def local(queries, new_kv, pool, page_table, ctx_len, move_page, move_dest, append_page):
    fresh = new_kv[0]
    q = queries[0]
    mig, *parts = pack(page_table, ctx_len, move_page, move_dest, pool[0], fresh)
    mig = mig.reshape(INST * KVH, MOST * PAGE * 2, D)
    mig = lax.all_to_all(mig, ("ba", "y"), 0, 0, tiled=True)
    parts = [r.reshape(REST * 2, D) for r in parts]
    parts = [parts[0]] + [shift(parts[k], "y", k) for k in range(1, 4)]
    qs = [q] + [shift(q, "x", k) for k in range(1, 4)]
    out2, *shared = first(qs[2], mig.reshape(MIG_ROWS // 128, 256, D), parts)
    got2 = back(out2, 2)
    out1, out3 = more((qs[1], qs[3]), *shared)
    got1, got3 = back(out1, 1), back(out3, 3)
    (out0,) = more((q,), *shared)
    updated = append(append_page, out3, pool[0], fresh)
    return combine([out0, got1, got2, got3])[None], updated[None]


def solution(mesh):
    grid = Mesh(np.asarray(mesh.devices).reshape(4, 4, 8), ("y", "x", "ba"))
    aa = ("y", "x")
    return jax.shard_map(
        local,
        mesh=grid,
        in_specs=(
            P("ba", None, aa),
            P("ba", aa, None, None),
            P("ba", aa, None, None, None),
            P("ba", aa),
            P("ba", aa),
            P("ba", aa),
            P("ba", aa),
            P("ba", aa),
        ),
        out_specs=(P("ba", None, aa), P("ba", aa, None, None, None)),
        check_vma=False,
    )
```

```python
import functools
import math

import jax
import jax.numpy as jnp
import numpy as np
from jax import lax
from jax.experimental import pallas as pl
from jax.experimental.pallas import tpu as pltpu
from jax.sharding import Mesh, PartitionSpec as P

D = 128
KVH = 4
MOST = 2
PAGE = 32
TABLE = 4
MOVES = 7
INST = 8
NEW_DEV = 8
NQ = 128
RES = TABLE * PAGE + NEW_DEV
DEAD = 128.0
BIG = -1e30
BF = jnp.bfloat16
F32 = jnp.float32
F16 = jnp.float16
LOG_SCALE = math.log2(math.e) / math.sqrt(D)
HALF = MOST * PAGE
REST = RES - HALF
MIG_ROWS = INST * KVH * MOST * PAGE
OLD_ROWS = (TABLE - MOST) * PAGE * KVH
ROWS = MIG_ROWS + OLD_ROWS + 128
CHUNK = 256

SMEM = pl.BlockSpec(memory_space=pltpu.SMEM)
HBM = pl.BlockSpec(memory_space=pltpu.HBM)
VMEM = pl.BlockSpec(memory_space=pltpu.VMEM)


def here():
    return (
        lax.axis_index("x").astype(jnp.int32),
        lax.axis_index("y").astype(jnp.int32),
        lax.axis_index("ba").astype(jnp.int32),
    )


def pack_kernel(
    table_in, ctx_in, page_in, dest_in, source, new, mig, r0, r1, r2, r3, table, ctx, page, dest,
    pool, dead, sem_s, sem_p, sem_m, sem_r
):
    fetch = pltpu.make_async_copy(source, pool, sem_p)
    fetch.start()
    scalars = [
        pltpu.make_async_copy(a, b, sem_s.at[i])
        for i, (a, b) in enumerate(
            ((table_in, table), (ctx_in, ctx), (page_in, page), (dest_in, dest))
        )
    ]
    for copy in scalars:
        copy.start()
    dead[...] = jnp.full_like(dead, DEAD)
    _, y_here, b_here = here()
    for copy in scalars:
        copy.wait()
    for d in range(INST):
        count = jnp.int32(0)
        for m in range(MOVES):
            count += (dest[0, m] == d).astype(jnp.int32)
        for s in range(MOST):

            @pl.when((count <= s) & (b_here != d))
            def _():
                pltpu.make_async_copy(dead, mig.at[d, :, s], sem_m).start()

    fetch.wait()
    for m in range(MOVES):
        rank = jnp.int32(0)
        for e in range(m):
            rank += (dest[0, e] == dest[0, m]).astype(jnp.int32)
        for y in range(KVH):
            pltpu.make_async_copy(
                pool.at[page[0, m], :, :, pl.ds(y * D, D)], mig.at[dest[0, m], y, rank], sem_m
            ).start()
    index = lax.broadcasted_iota(jnp.int32, (PAGE, 2, KVH * D), 0)
    for j in range(TABLE):
        page_j = table[0, j]

        @pl.when(ctx[0, 0] < (j + 1) * PAGE)
        def _():
            rows = pool[page_j].astype(F32)
            alive = index < ctx[0, 0] - j * PAGE
            pool[page_j] = jnp.where(alive, rows, DEAD).astype(BF)

    outs = (r0, r1, r2, r3)
    for k in range(4):
        lanes = pl.ds(pl.multiple_of(lax.rem(y_here + k, 4) * D, D), D)
        for j in range(MOST, TABLE):
            pltpu.make_async_copy(
                pool.at[table[0, j], :, :, lanes],
                outs[k].at[pl.ds((j - MOST) * PAGE, PAGE)],
                sem_r.at[k],
            ).start()
        pltpu.make_async_copy(
            new.at[:, :, lanes], outs[k].at[pl.ds((TABLE - MOST) * PAGE, NEW_DEV)], sem_r.at[k]
        ).start()
    for j in range(MOST):
        for y in range(KVH):
            pltpu.make_async_copy(
                pool.at[table[0, j], :, :, pl.ds(y * D, D)], mig.at[b_here, y, j], sem_m
            ).start()
    for k in range(4):
        pltpu.make_async_copy(outs[k], outs[k], sem_r.at[k]).wait()
    pltpu.make_async_copy(mig, mig, sem_m).wait()


def pack(table, ctx, page, dest, pool, new):
    return pl.pallas_call(
        pack_kernel,
        in_specs=[HBM, VMEM, HBM, HBM, HBM, VMEM],
        out_specs=[HBM] * 5,
        out_shape=[jax.ShapeDtypeStruct((INST, KVH, MOST, PAGE, 2, D), BF)]
        + [jax.ShapeDtypeStruct((REST, 2, D), BF)] * 4,
        scratch_shapes=[pltpu.SMEM(a.shape, jnp.int32) for a in (table, ctx, page, dest)]
        + [
            pltpu.VMEM(pool.shape, BF),
            pltpu.VMEM((KVH, PAGE, 2, D), BF),
            pltpu.SemaphoreType.DMA((4,)),
            pltpu.SemaphoreType.DMA,
            pltpu.SemaphoreType.DMA,
            pltpu.SemaphoreType.DMA((4,)),
        ],
        compiler_params=pltpu.CompilerParams(vmem_limit_bytes=60 << 20),
        name="pack",
    )(table, ctx, page, dest, pool, new)


def append_kernel(page_in, after, source, new, target, page, pool, sem):
    copy = pltpu.make_async_copy(source, pool, sem.at[0])
    copy.start()
    scalar = pltpu.make_async_copy(page_in, page, sem.at[1])
    scalar.start()
    scalar.wait()
    copy.wait()
    last = pltpu.make_async_copy(new, pool.at[page[0, 0], pl.ds(0, NEW_DEV)], sem.at[1])
    last.start()
    last.wait()
    copy = pltpu.make_async_copy(pool, target, sem.at[0])
    copy.start()
    copy.wait()


def append(page, after, pool, new):
    return pl.pallas_call(
        append_kernel,
        in_specs=[HBM] * 4,
        out_specs=HBM,
        out_shape=jax.ShapeDtypeStruct(pool.shape, BF),
        scratch_shapes=[
            pltpu.SMEM((1, 1), jnp.int32),
            pltpu.VMEM(pool.shape, BF),
            pltpu.SemaphoreType.DMA((2,)),
        ],
        compiler_params=pltpu.CompilerParams(vmem_limit_bytes=8 << 20),
        cost_estimate=cost(1),
        name="append",
    )(page, after, pool, new)


def pickers():
    row = lax.broadcasted_iota(jnp.int32, (256, 128), 0)
    col = lax.broadcasted_iota(jnp.int32, (256, 128), 1)
    keys = (row == 2 * col).astype(BF)
    row = lax.broadcasted_iota(jnp.int32, (128, 256), 0)
    col = lax.broadcasted_iota(jnp.int32, (128, 256), 1)
    return keys, (col == 2 * row + 1).astype(BF)


def put(x, pick, kt, vv, at):
    keys = lax.dot_general(x, pick[0], (((0,), (0,)), ((), ())), preferred_element_type=F32)
    kt[0:128, at] = keys.astype(BF)
    sub = lax.broadcasted_iota(jnp.int32, (128, 128), 0)
    kt[128:256, at] = jnp.where((sub == 0) & (keys > 64.0), BIG, 0.0).astype(BF)
    vals = jnp.dot(pick[1], x, preferred_element_type=F32)
    vv[at, 0:128] = vals.astype(BF)
    vv[at, 128:256] = jnp.ones((128, 128), BF)


def fill(mig, parts, kt, vv, aug):
    x_here, y_here, _ = here()
    pick = pickers()
    for i in range(MIG_ROWS // 128):
        put(mig[i], pick, kt, vv, slice(i * 128, i * 128 + 128))
    for i in range(2):
        x = jnp.concatenate([parts[2 * i][0:128], parts[2 * i + 1][0:128]], axis=0)
        at = MIG_ROWS + i * 128
        put(x, pick, kt, vv, slice(at, at + 128))
    at = MIG_ROWS + OLD_ROWS
    fresh = [r[128:144] for r in parts] + [jnp.zeros((192, 128), BF)]
    put(jnp.concatenate(fresh, axis=0), pick, kt, vv, slice(at, at + 128))
    sub = lax.broadcasted_iota(jnp.int32, (128, 128), 0)
    lane = lax.broadcasted_iota(jnp.int32, (128, 128), 1)
    hot = jnp.where((sub == 1 + lane) & (lane < 32), 1.0, 0.0)
    kt[128:256, at : at + 128] = jnp.where((sub == 0) & (lane >= 32), BIG, hot).astype(BF)
    j = lane - 1
    source = (y_here + 4 - (j >> 3)) & 3
    pos = source * 32 + x_here * 8 + (j & 7)
    bar = jnp.where((lane >= 1) & (lane < 33) & (pos > sub), BIG, 0.0)
    aug[...] = jnp.where(lane == 0, 1.0, bar).astype(BF)


def rows_of(qs, outs, kt, vv, aug, s_ref):
    per = CHUNK // 128
    units = [(i, c) for i in range(len(qs)) for c in range(512 // CHUNK)]
    lane = lax.broadcasted_iota(jnp.int32, (128, 128), 1)
    stats = [jnp.zeros((128, 128), F32) for _ in qs]

    def score(u):
        i, c = units[u]
        q = [
            jnp.concatenate([qs[i][:, (c * per + h) * 128 : (c * per + h + 1) * 128], aug[...]], 1)
            for h in range(per)
        ]
        s_ref[u % 2] = jnp.dot(jnp.concatenate(q, 0), kt[...], preferred_element_type=F32)

    score(0)
    for u, (i, c) in enumerate(units):
        if u + 1 < len(units):
            score(u + 1)
        s = s_ref[u % 2]
        top = jnp.max(s, axis=1, keepdims=True)
        p = jnp.exp2((s - top) * LOG_SCALE)
        high = p.astype(BF)
        low = (p - high.astype(F32)).astype(BF)
        o = jnp.dot(high, vv[...], preferred_element_type=F32)
        o += jnp.dot(low, vv[...], preferred_element_type=F32)
        total = o[:, 128:]
        mean = o[:, :128] / total
        most = jnp.maximum(jnp.max(jnp.abs(mean), axis=1, keepdims=True), 1e-30)
        mean = mean / most
        lse = jnp.log2(total) + top * LOG_SCALE
        num = lse + jnp.log2(most)
        for h in range(per):
            part = slice(h * 128, h * 128 + 128)
            at = c * per + h
            outs[i][0:128, at * 128 : at * 128 + 128] = mean[part]
            stats[i] = jnp.where(lane == at, lse[part], stats[i])
            stats[i] = jnp.where(lane == 4 + at, num[part], stats[i])
    for i, out in enumerate(outs):
        rows = stats[i].T[0:8]
        high = jnp.floor(rows * 2.0 + 0.5) * 0.5
        out[128:136, 0:128] = high
        out[128:136, 128:256] = rows - high
        out[128:136, 256:512] = jnp.zeros((8, 256), F32)


def first_kernel(q, mig, r0, r1, r2, r3, out, kt, vv, aug, s_ref):
    fill(mig, (r0, r1, r2, r3), kt, vv, aug)
    rows_of((q,), (out,), kt, vv, aug, s_ref)


def more_kernel(count, *refs):
    *qs, kt, vv, aug = refs[: count + 3]
    rows_of(qs, refs[-1 - count : -1], kt, vv, aug, refs[-1])


def cost(count):
    return pl.CostEstimate(
        flops=count << 20, transcendentals=count << 10, bytes_accessed=count << 16
    )


PART = jax.ShapeDtypeStruct((136, 512), F32)
SCORES = pltpu.VMEM((2, CHUNK, ROWS), F32)


def first(q, mig, parts):
    return pl.pallas_call(
        first_kernel,
        in_specs=[VMEM] * 6,
        out_specs=[VMEM] * 4,
        out_shape=[
            PART,
            jax.ShapeDtypeStruct((256, ROWS), BF),
            jax.ShapeDtypeStruct((ROWS, 256), BF),
            jax.ShapeDtypeStruct((128, 128), BF),
        ],
        scratch_shapes=[SCORES],
        compiler_params=pltpu.CompilerParams(vmem_limit_bytes=28 << 20),
        cost_estimate=cost(1),
        name="first",
    )(q, mig, *parts)


def more(qs, kt, vv, aug, after=None):
    late = () if after is None else (after,)
    return pl.pallas_call(
        functools.partial(more_kernel, len(qs)),
        in_specs=[VMEM] * (len(qs) + 3) + [HBM] * len(late),
        out_specs=[VMEM] * len(qs),
        out_shape=[PART] * len(qs),
        scratch_shapes=[SCORES],
        compiler_params=pltpu.CompilerParams(vmem_limit_bytes=28 << 20),
        cost_estimate=cost(len(qs)),
        name="more",
    )(*qs, kt, vv, aug, *late)


def combine_kernel(g0, g2, g, out):
    parts = (g0, g2, g.at[0], g.at[1])
    stats = [g[128:136, 0:128] + g[128:136, 128:256] for g in parts]
    dens = [x[0:4] for x in stats]
    top = functools.reduce(jnp.maximum, dens)
    share = 1.0 / sum(jnp.exp2(x - top) for x in dens)
    rows = [jnp.exp2(x[4:8] - top) * share for x in stats]
    cols = jnp.concatenate(rows + [jnp.zeros((112, 128), F32)], axis=0).T
    for h in range(4):
        lanes = slice(h * 128, h * 128 + 128)
        result = sum(
            g[0:128, lanes] * cols[:, 4 * k + h : 4 * k + h + 1] for k, g in enumerate(parts)
        )
        out[:, lanes] = result.astype(BF)


def combine(*parts):
    return pl.pallas_call(
        combine_kernel,
        in_specs=[VMEM] * 3,
        out_specs=VMEM,
        out_shape=jax.ShapeDtypeStruct((128, 512), BF),
        compiler_params=pltpu.CompilerParams(vmem_limit_bytes=8 << 20),
        name="combine",
    )(*parts)


def shift(value, axis, k):
    return lax.ppermute(value, axis, [(i, (i + k) % 4) for i in range(4)])


def swap(value, k):
    return lax.ppermute(value, "x", [(i, i ^ k) for i in range(4)])


def local(queries, new_kv, pool, page_table, ctx_len, move_page, move_dest, append_page):
    fresh = new_kv[0]
    q = queries[0]
    mig, *parts = pack(page_table, ctx_len, move_page, move_dest, pool[0], fresh)
    mig = mig.reshape(INST * KVH, MOST * PAGE * 2, D)
    mig = lax.all_to_all(mig, ("ba", "y"), 0, 0, tiled=True)
    parts = [r.reshape(REST * 2, D) for r in parts]
    parts = [parts[0]] + [shift(parts[k], "y", k) for k in range(1, 4)]
    q2 = swap(q, 2)
    pair = swap(jnp.concatenate([q, q2], axis=0), 1)
    qs = [q, pair[:128], q2, pair[128:]]
    out2, *shared = first(qs[2], mig.reshape(MIG_ROWS // 128, 256, D), parts)
    got2 = swap(out2.astype(F16), 2).astype(F32)
    out1, out3 = more((qs[1], qs[3]), *shared)
    sent = [swap(out.astype(F16), k) for k, out in ((1, out1), (3, out3))]
    got = jnp.stack(sent).astype(F32)
    (out0,) = more((q,), *shared, after=got2)
    updated = append(append_page, out3, pool[0], fresh)
    return combine(out0, got2, got)[None], updated[None]


def solution(mesh):
    grid = Mesh(np.asarray(mesh.devices).reshape(4, 4, 8), ("y", "x", "ba"))
    aa = ("y", "x")
    return jax.shard_map(
        local,
        mesh=grid,
        in_specs=(
            P("ba", None, aa),
            P("ba", aa, None, None),
            P("ba", aa, None, None, None),
            P("ba", aa),
            P("ba", aa),
            P("ba", aa),
            P("ba", aa),
            P("ba", aa),
        ),
        out_specs=(P("ba", None, aa), P("ba", aa, None, None, None)),
        check_vma=False,
    )
```

```python
import functools
import math

import jax
import jax.numpy as jnp
import numpy as np
from jax import lax
from jax.experimental import pallas as pl
from jax.experimental.pallas import tpu as pltpu
from jax.sharding import Mesh, PartitionSpec as P

D = 128
KVH = 4
MOST = 2
PAGE = 32
TABLE = 4
MOVES = 7
INST = 8
NEW_DEV = 8
NQ = 128
RES = TABLE * PAGE + NEW_DEV
DEAD = 128.0
BIG = -1e30
BF = jnp.bfloat16
F32 = jnp.float32
F16 = jnp.float16
LOG_SCALE = math.log2(math.e) / math.sqrt(D)
HALF = MOST * PAGE
REST = RES - HALF
MIG_ROWS = INST * KVH * MOST * PAGE
OLD_ROWS = (TABLE - MOST) * PAGE * KVH
ROWS = MIG_ROWS + OLD_ROWS + 128
SPANS = (0, 1280, ROWS)

SMEM = pl.BlockSpec(memory_space=pltpu.SMEM)
HBM = pl.BlockSpec(memory_space=pltpu.HBM)
VMEM = pl.BlockSpec(memory_space=pltpu.VMEM)


def here():
    return (
        lax.axis_index("x").astype(jnp.int32),
        lax.axis_index("y").astype(jnp.int32),
        lax.axis_index("ba").astype(jnp.int32),
    )


def pack_kernel(
    table_in, ctx_in, page_in, dest_in, source, new, mig, r0, r1, r2, r3, table, ctx, page, dest,
    pool, dead, sem_s, sem_p, sem_m, sem_r
):
    fetch = pltpu.make_async_copy(source, pool, sem_p)
    fetch.start()
    scalars = [
        pltpu.make_async_copy(a, b, sem_s.at[i])
        for i, (a, b) in enumerate(
            ((table_in, table), (ctx_in, ctx), (page_in, page), (dest_in, dest))
        )
    ]
    for copy in scalars:
        copy.start()
    dead[...] = jnp.full_like(dead, DEAD)
    _, y_here, b_here = here()
    for copy in scalars:
        copy.wait()
    for d in range(INST):
        count = jnp.int32(0)
        for m in range(MOVES):
            count += (dest[0, m] == d).astype(jnp.int32)
        for s in range(MOST):

            @pl.when((count <= s) & (b_here != d))
            def _():
                pltpu.make_async_copy(dead, mig.at[d, :, s], sem_m).start()

    fetch.wait()
    for m in range(MOVES):
        rank = jnp.int32(0)
        for e in range(m):
            rank += (dest[0, e] == dest[0, m]).astype(jnp.int32)
        for y in range(KVH):
            pltpu.make_async_copy(
                pool.at[page[0, m], :, :, pl.ds(y * D, D)], mig.at[dest[0, m], y, rank], sem_m
            ).start()
    index = lax.broadcasted_iota(jnp.int32, (PAGE, 2, KVH * D), 0)
    for j in range(TABLE):
        page_j = table[0, j]

        @pl.when(ctx[0, 0] < (j + 1) * PAGE)
        def _():
            rows = pool[page_j].astype(F32)
            alive = index < ctx[0, 0] - j * PAGE
            pool[page_j] = jnp.where(alive, rows, DEAD).astype(BF)

    outs = (r0, r1, r2, r3)
    for k in range(4):
        lanes = pl.ds(pl.multiple_of(lax.rem(y_here + k, 4) * D, D), D)
        for j in range(MOST, TABLE):
            pltpu.make_async_copy(
                pool.at[table[0, j], :, :, lanes],
                outs[k].at[pl.ds((j - MOST) * PAGE, PAGE)],
                sem_r.at[k],
            ).start()
        pltpu.make_async_copy(
            new.at[:, :, lanes], outs[k].at[pl.ds((TABLE - MOST) * PAGE, NEW_DEV)], sem_r.at[k]
        ).start()
    for j in range(MOST):
        for y in range(KVH):
            pltpu.make_async_copy(
                pool.at[table[0, j], :, :, pl.ds(y * D, D)], mig.at[b_here, y, j], sem_m
            ).start()
    for k in range(4):
        pltpu.make_async_copy(outs[k], outs[k], sem_r.at[k]).wait()
    pltpu.make_async_copy(mig, mig, sem_m).wait()


def pack(table, ctx, page, dest, pool, new):
    return pl.pallas_call(
        pack_kernel,
        in_specs=[HBM, VMEM, HBM, HBM, HBM, VMEM],
        out_specs=[HBM] * 5,
        out_shape=[jax.ShapeDtypeStruct((INST, KVH, MOST, PAGE, 2, D), BF)]
        + [jax.ShapeDtypeStruct((REST, 2, D), BF)] * 4,
        scratch_shapes=[pltpu.SMEM(a.shape, jnp.int32) for a in (table, ctx, page, dest)]
        + [
            pltpu.VMEM(pool.shape, BF),
            pltpu.VMEM((KVH, PAGE, 2, D), BF),
            pltpu.SemaphoreType.DMA((4,)),
            pltpu.SemaphoreType.DMA,
            pltpu.SemaphoreType.DMA,
            pltpu.SemaphoreType.DMA((4,)),
        ],
        compiler_params=pltpu.CompilerParams(vmem_limit_bytes=60 << 20),
        name="pack",
    )(table, ctx, page, dest, pool, new)


def append_kernel(page_in, after, source, new, target, page, pool, sem):
    copy = pltpu.make_async_copy(source, pool, sem.at[0])
    copy.start()
    scalar = pltpu.make_async_copy(page_in, page, sem.at[1])
    scalar.start()
    scalar.wait()
    copy.wait()
    last = pltpu.make_async_copy(new, pool.at[page[0, 0], pl.ds(0, NEW_DEV)], sem.at[1])
    last.start()
    last.wait()
    copy = pltpu.make_async_copy(pool, target, sem.at[0])
    copy.start()
    copy.wait()


def append(page, after, pool, new):
    return pl.pallas_call(
        append_kernel,
        in_specs=[HBM] * 4,
        out_specs=HBM,
        out_shape=jax.ShapeDtypeStruct(pool.shape, BF),
        scratch_shapes=[
            pltpu.SMEM((1, 1), jnp.int32),
            pltpu.VMEM(pool.shape, BF),
            pltpu.SemaphoreType.DMA((2,)),
        ],
        compiler_params=pltpu.CompilerParams(vmem_limit_bytes=8 << 20),
        cost_estimate=cost(1),
        name="append",
    )(page, after, pool, new)


def put(x, pick, kk, vt, at, marks=None):
    lane = lax.broadcasted_iota(jnp.int32, (128, 128), 1)
    keys = jnp.dot(pick[0], x, preferred_element_type=F32)
    kk[at, 0:128] = keys.astype(BF)
    if marks is None:
        marks = jnp.where((lane == 0) & (keys > 64.0), BIG, 0.0)
    kk[at, 128:256] = marks.astype(BF)
    vals = lax.dot_general(x, pick[1], (((0,), (0,)), ((), ())), preferred_element_type=F32)
    vt[0:128, at] = vals.astype(BF)


def fill(mig, parts, kk, vt):
    row = lax.broadcasted_iota(jnp.int32, (128, 256), 0)
    col = lax.broadcasted_iota(jnp.int32, (128, 256), 1)
    keys = (col == 2 * row).astype(BF)
    row = lax.broadcasted_iota(jnp.int32, (256, 128), 0)
    col = lax.broadcasted_iota(jnp.int32, (256, 128), 1)
    pick = (keys, (row == 2 * col + 1).astype(BF))
    vt[128:144, :] = jnp.ones((16, ROWS), BF)
    for i in range(MIG_ROWS // 128):
        put(mig[i], pick, kk, vt, slice(i * 128, i * 128 + 128))
    for i in range(2):
        x = jnp.concatenate([parts[2 * i][0:128], parts[2 * i + 1][0:128]], axis=0)
        at = MIG_ROWS + i * 128
        put(x, pick, kk, vt, slice(at, at + 128))
    at = MIG_ROWS + OLD_ROWS
    x = jnp.concatenate([r[128:144] for r in parts] + [jnp.zeros((192, 128), BF)], axis=0)
    sub = lax.broadcasted_iota(jnp.int32, (128, 128), 0)
    lane = lax.broadcasted_iota(jnp.int32, (128, 128), 1)
    hot = jnp.where((lane == 1 + sub) & (sub < 32), 1.0, 0.0)
    marks = jnp.where((lane == 0) & (sub >= 32), BIG, hot)
    put(x, pick, kk, vt, slice(at, at + 128), marks)


def turn_kernel(q0, q2, pair, out):
    x_here, y_here, _ = here()
    sub = lax.broadcasted_iota(jnp.int32, (128, 128), 0)
    lane = lax.broadcasted_iota(jnp.int32, (128, 128), 1)
    j = sub - 1
    source = (y_here + 4 - (j >> 3)) & 3
    pos = source * 32 + x_here * 8 + (j & 7)
    bar = jnp.where((sub >= 1) & (sub < 33) & (pos > lane), BIG, 0.0)
    aug = jnp.where(sub == 0, 1.0, bar).astype(BF)
    for k, q in enumerate((q0, pair.at[0:128], q2, pair.at[128:256])):
        for h in range(4):
            lanes = slice(h * 128, h * 128 + 128)
            out[k, 0:128, lanes] = q[:, lanes].astype(F32).T.astype(BF)
            out[k, 128:256, lanes] = aug


def turn(q, q2, pair):
    return pl.pallas_call(
        turn_kernel,
        in_specs=[VMEM] * 3,
        out_specs=VMEM,
        out_shape=jax.ShapeDtypeStruct((4, 256, 512), BF),
        compiler_params=pltpu.CompilerParams(vmem_limit_bytes=8 << 20),
        cost_estimate=cost(1),
        name="turn",
    )(q, q2, pair)


def attend(ks, outs, qt, kk, vt, s_ref):
    units = [(i, t) for i in range(len(ks)) for t in range(len(SPANS) - 1)]

    def score(u):
        i, t = units[u]
        rows = slice(SPANS[t], SPANS[t + 1])
        size = SPANS[t + 1] - SPANS[t]
        s_ref[u % 2, 0:size] = jnp.dot(kk[rows], qt[ks[i]], preferred_element_type=F32)

    score(0)
    for u, (i, t) in enumerate(units):
        if u + 1 < len(units):
            score(u + 1)
        rows = slice(SPANS[t], SPANS[t + 1])
        s = s_ref[u % 2, 0 : SPANS[t + 1] - SPANS[t]]
        top = jnp.max(s, axis=0, keepdims=True)
        p = jnp.exp2((s - top) * LOG_SCALE)
        high = p.astype(BF)
        low = (p - high.astype(F32)).astype(BF)
        o = jnp.dot(vt[:, rows], high, preferred_element_type=F32)
        o += jnp.dot(vt[:, rows], low, preferred_element_type=F32)
        if t == 0:
            best, sums = top, o
        else:
            both = jnp.maximum(best, top)
            sums = sums * jnp.exp2((best - both) * LOG_SCALE) + o * jnp.exp2((top - both) * LOG_SCALE)
            best = both
        if t + 2 < len(SPANS):
            continue
        total = sums[128:129]
        mean = sums[0:128] / total
        most = jnp.maximum(jnp.max(jnp.abs(mean), axis=0, keepdims=True), 1e-30)
        den = jnp.log2(total) + best * LOG_SCALE
        num = den + jnp.log2(most)
        outs[i][0:128] = mean / most
        rows = []
        for x in (den, num):
            high = jnp.floor(x * 2.0 + 0.5) * 0.5
            rows += [high, x - high]
        outs[i][128:136] = jnp.concatenate(rows + [jnp.zeros((4, 512), F32)], axis=0)


def first_kernel(k, qt, mig, r0, r1, r2, r3, out, kk, vt, s_ref):
    fill(mig, (r0, r1, r2, r3), kk, vt)
    attend((k,), (out,), qt, kk, vt, s_ref)


def more_kernel(ks, qt, kk, vt, *refs):
    attend(ks, refs[-1 - len(ks) : -1], qt, kk, vt, refs[-1])


def cost(count):
    return pl.CostEstimate(
        flops=count << 20, transcendentals=count << 10, bytes_accessed=count << 16
    )


PART = jax.ShapeDtypeStruct((136, 512), F32)
SCORES = pltpu.VMEM((2, max(b - a for a, b in zip(SPANS, SPANS[1:])), 512), F32)


def first(k, qt, mig, parts):
    return pl.pallas_call(
        functools.partial(first_kernel, k),
        in_specs=[VMEM] * 6,
        out_specs=[VMEM] * 3,
        out_shape=[
            PART,
            jax.ShapeDtypeStruct((ROWS, 256), BF),
            jax.ShapeDtypeStruct((144, ROWS), BF),
        ],
        scratch_shapes=[SCORES],
        compiler_params=pltpu.CompilerParams(vmem_limit_bytes=28 << 20),
        cost_estimate=cost(1),
        name="first",
    )(qt, mig, *parts)


def more(ks, qt, kk, vt, after=None):
    late = () if after is None else (after,)
    return pl.pallas_call(
        functools.partial(more_kernel, ks),
        in_specs=[VMEM] * 3 + [HBM] * len(late),
        out_specs=[VMEM] * len(ks),
        out_shape=[PART] * len(ks),
        scratch_shapes=[SCORES],
        compiler_params=pltpu.CompilerParams(vmem_limit_bytes=28 << 20),
        cost_estimate=cost(len(ks)),
        name="more",
    )(qt, kk, vt, *late)


def combine_kernel(g0, g2, g, out):
    parts = (g0, g2, g.at[0], g.at[1])
    dens = [x[128:129] + x[129:130] for x in parts]
    top = functools.reduce(jnp.maximum, dens)
    share = 1.0 / sum(jnp.exp2(x - top) for x in dens)
    result = sum(
        x[0:128] * (jnp.exp2(x[130:131] + x[131:132] - top) * share) for x in parts
    )
    for h in range(4):
        lanes = slice(h * 128, h * 128 + 128)
        out[:, lanes] = result[:, lanes].T.astype(BF)


def combine(*parts):
    return pl.pallas_call(
        combine_kernel,
        in_specs=[VMEM] * 3,
        out_specs=VMEM,
        out_shape=jax.ShapeDtypeStruct((128, 512), BF),
        compiler_params=pltpu.CompilerParams(vmem_limit_bytes=8 << 20),
        name="combine",
    )(*parts)


def shift(value, axis, k):
    return lax.ppermute(value, axis, [(i, (i + k) % 4) for i in range(4)])


def swap(value, k):
    return lax.ppermute(value, "x", [(i, i ^ k) for i in range(4)])


def local(queries, new_kv, pool, page_table, ctx_len, move_page, move_dest, append_page):
    fresh = new_kv[0]
    q = queries[0]
    mig, *parts = pack(page_table, ctx_len, move_page, move_dest, pool[0], fresh)
    mig = mig.reshape(INST * KVH, MOST * PAGE * 2, D)
    mig = lax.all_to_all(mig, ("ba", "y"), 0, 0, tiled=True)
    parts = [r.reshape(REST * 2, D) for r in parts]
    parts = [parts[0]] + [shift(parts[k], "y", k) for k in range(1, 4)]
    q2 = swap(q, 2)
    updated = append(append_page, parts[0], pool[0], fresh)
    far, updated = lax.optimization_barrier((q2, updated))
    pair = swap(jnp.concatenate([q, far], axis=0), 1)
    qt = turn(q, q2, pair)
    out2, kk, vt = first(2, qt, mig.reshape(MIG_ROWS // 128, 256, D), parts)
    got2 = swap(out2.astype(F16), 2).astype(F32)
    out1, out3 = more((1, 3), qt, kk, vt)
    sent = [swap(out.astype(F16), k) for k, out in ((1, out1), (3, out3))]
    got = jnp.stack(sent).astype(F32)
    (out0,) = more((0,), qt, kk, vt, after=got2)
    return combine(out0, got2, got)[None], updated[None]


def solution(mesh):
    grid = Mesh(np.asarray(mesh.devices).reshape(4, 4, 8), ("y", "x", "ba"))
    aa = ("y", "x")
    return jax.shard_map(
        local,
        mesh=grid,
        in_specs=(
            P("ba", None, aa),
            P("ba", aa, None, None),
            P("ba", aa, None, None, None),
            P("ba", aa),
            P("ba", aa),
            P("ba", aa),
            P("ba", aa),
            P("ba", aa),
        ),
        out_specs=(P("ba", None, aa), P("ba", aa, None, None, None)),
        check_vma=False,
    )
```

```python
import functools
import math

import jax
import jax.numpy as jnp
import numpy as np
from jax import lax
from jax.experimental import pallas as pl
from jax.experimental.pallas import tpu as pltpu
from jax.sharding import Mesh, PartitionSpec as P

D = 128
KVH = 4
MOST = 2
PAGE = 32
TABLE = 4
MOVES = 7
INST = 8
NEW_DEV = 8
NQ = 128
RES = TABLE * PAGE + NEW_DEV
DEAD = 128.0
BIG = -1e30
BF = jnp.bfloat16
F32 = jnp.float32
F16 = jnp.float16
LOG_SCALE = math.log2(math.e) / math.sqrt(D)
HALF = MOST * PAGE
REST = RES - HALF
MIG_ROWS = INST * KVH * MOST * PAGE
OLD_ROWS = (TABLE - MOST) * PAGE * KVH
ROWS = MIG_ROWS + OLD_ROWS + 128
WIDE = (0, 1280, ROWS)
NARROW = (0, 640, 1280, 1920, ROWS)

SMEM = pl.BlockSpec(memory_space=pltpu.SMEM)
HBM = pl.BlockSpec(memory_space=pltpu.HBM)
VMEM = pl.BlockSpec(memory_space=pltpu.VMEM)


def here():
    return (
        lax.axis_index("x").astype(jnp.int32),
        lax.axis_index("y").astype(jnp.int32),
        lax.axis_index("ba").astype(jnp.int32),
    )


def pack_kernel(
    table_in, page_in, dest_in, source, mig, table, page, dest, pool, dead, sem_s, sem_p, sem_m
):
    fetch = pltpu.make_async_copy(source, pool, sem_p)
    fetch.start()
    scalars = [
        pltpu.make_async_copy(a, b, sem_s.at[i])
        for i, (a, b) in enumerate(((table_in, table), (page_in, page), (dest_in, dest)))
    ]
    for copy in scalars:
        copy.start()
    dead[...] = jnp.full_like(dead, DEAD)
    b_here = here()[2]
    for copy in scalars:
        copy.wait()
    for d in range(INST):
        count = jnp.int32(0)
        for m in range(MOVES):
            count += (dest[0, m] == d).astype(jnp.int32)
        for s in range(MOST):

            @pl.when((count <= s) & (b_here != d))
            def _():
                pltpu.make_async_copy(dead, mig.at[d, :, s], sem_m).start()

    fetch.wait()
    for m in range(MOVES):
        rank = jnp.int32(0)
        for e in range(m):
            rank += (dest[0, e] == dest[0, m]).astype(jnp.int32)
        for y in range(KVH):
            pltpu.make_async_copy(
                pool.at[page[0, m], :, :, pl.ds(y * D, D)], mig.at[dest[0, m], y, rank], sem_m
            ).start()
    for j in range(MOST):
        for y in range(KVH):
            pltpu.make_async_copy(
                pool.at[table[0, j], :, :, pl.ds(y * D, D)], mig.at[b_here, y, j], sem_m
            ).start()
    pltpu.make_async_copy(mig, mig, sem_m).wait()


def pack(table, page, dest, pool):
    return pl.pallas_call(
        pack_kernel,
        in_specs=[HBM] * 4,
        out_specs=HBM,
        out_shape=jax.ShapeDtypeStruct((INST, KVH, MOST, PAGE, 2, D), BF),
        scratch_shapes=[pltpu.SMEM(a.shape, jnp.int32) for a in (table, page, dest)]
        + [
            pltpu.VMEM(pool.shape, BF),
            pltpu.VMEM((KVH, PAGE, 2, D), BF),
            pltpu.SemaphoreType.DMA((3,)),
            pltpu.SemaphoreType.DMA,
            pltpu.SemaphoreType.DMA,
        ],
        compiler_params=pltpu.CompilerParams(vmem_limit_bytes=60 << 20),
        name="pack",
    )(table, page, dest, pool)


def settle_kernel(
    table, ctx, page, after, source, new, r0, r1, r2, r3, target, pool, sem, sem_r
):
    fetch = pltpu.make_async_copy(source, pool, sem.at[0])
    fetch.start()
    y_here = here()[1]
    length = ctx[0, 0].astype(F32)
    fetch.wait()
    outs = (r0, r1, r2, r3)
    for k in range(4):
        lanes = pl.ds(pl.multiple_of(lax.rem(y_here + k, 4) * D, D), D)
        for j in range(MOST, TABLE):
            pltpu.make_async_copy(
                pool.at[table[0, j], :, :, lanes],
                outs[k].at[pl.ds((j - MOST) * PAGE, PAGE)],
                sem_r.at[k],
            ).start()
        outs[k][REST : REST + 4] = jnp.full((4, 2, D), length, F32).astype(BF)
        pltpu.make_async_copy(
            new.at[:, :, lanes], outs[k].at[pl.ds((TABLE - MOST) * PAGE, NEW_DEV)], sem_r.at[k]
        ).start()
    for k in range(4):
        moved = outs[k].at[pl.ds(0, REST)]
        pltpu.make_async_copy(moved, moved, sem_r.at[k]).wait()
    last = pltpu.make_async_copy(new, pool.at[page[0, 0], pl.ds(0, NEW_DEV)], sem.at[0])
    last.start()
    last.wait()
    copy = pltpu.make_async_copy(pool, target, sem.at[0])
    copy.start()
    copy.wait()


def settle(table, ctx, page, after, pool, new):
    return pl.pallas_call(
        settle_kernel,
        in_specs=[SMEM] * 3 + [HBM, HBM, VMEM],
        out_specs=[VMEM] * 4 + [HBM],
        out_shape=[jax.ShapeDtypeStruct((REST + 4, 2, D), BF)] * 4
        + [jax.ShapeDtypeStruct(pool.shape, BF)],
        scratch_shapes=[
            pltpu.VMEM(pool.shape, BF),
            pltpu.SemaphoreType.DMA((1,)),
            pltpu.SemaphoreType.DMA((4,)),
        ],
        compiler_params=pltpu.CompilerParams(vmem_limit_bytes=8 << 20),
        cost_estimate=cost(1),
        name="settle",
    )(table, ctx, page, after, pool, new)


def put(x, pick, kk, vt, at, marks=None):
    lane = lax.broadcasted_iota(jnp.int32, (128, 128), 1)
    keys = jnp.dot(pick[0], x, preferred_element_type=F32)
    kk[at, 0:128] = keys.astype(BF)
    if marks is None:
        marks = jnp.where((lane == 0) & (keys > 64.0), BIG, 0.0)
    kk[at, 128:256] = marks.astype(BF)
    vals = lax.dot_general(x, pick[1], (((0,), (0,)), ((), ())), preferred_element_type=F32)
    vt[0:128, at] = vals.astype(BF)


def fill(mig, parts, kk, vt):
    row = lax.broadcasted_iota(jnp.int32, (128, 256), 0)
    col = lax.broadcasted_iota(jnp.int32, (128, 256), 1)
    keys = (col == 2 * row).astype(BF)
    row = lax.broadcasted_iota(jnp.int32, (256, 128), 0)
    col = lax.broadcasted_iota(jnp.int32, (256, 128), 1)
    pick = (keys, (row == 2 * col + 1).astype(BF))
    vt[128:144, :] = jnp.ones((16, ROWS), BF)
    sub = lax.broadcasted_iota(jnp.int32, (128, 128), 0)
    lane = lax.broadcasted_iota(jnp.int32, (128, 128), 1)
    b_here = here()[2]
    live = [r[144:152].astype(F32)[0:1] for r in parts]
    row = sub.astype(F32)
    for i in range(MIG_ROWS // 128):
        source = lax.rem(b_here + 1 + (i >> 1), INST)
        x = mig[2 * source + (i & 1)]
        marks = None
        if i >= MIG_ROWS // 128 - 2:
            ctx = [live_of(live, 2 * (i & 1) + e) for e in range(2)]
            dead = row >= jnp.where(sub < 64, ctx[0], ctx[1] + 64.0)
            marks = jnp.where((lane == 0) & dead, BIG, 0.0)
        put(x, pick, kk, vt, slice(i * 128, i * 128 + 128), marks)
    for i in range(2):
        x = jnp.concatenate([parts[2 * i][0:128], parts[2 * i + 1][0:128]], axis=0)
        at = MIG_ROWS + i * 128
        dead = row >= jnp.where(sub < 64, live[2 * i] - 64.0, live[2 * i + 1])
        marks = jnp.where((lane == 0) & dead, BIG, 0.0)
        put(x, pick, kk, vt, slice(at, at + 128), marks)
    at = MIG_ROWS + OLD_ROWS
    x = jnp.concatenate([r[128:144] for r in parts] + [jnp.zeros((192, 128), BF)], axis=0)
    hot = jnp.where((lane == 1 + sub) & (sub < 32), 1.0, 0.0)
    marks = jnp.where((lane == 0) & (sub >= 32), BIG, hot)
    put(x, pick, kk, vt, slice(at, at + 128), marks)


def live_of(live, y):
    y_here = here()[1]
    value = live[0]
    for k in range(1, 4):
        value = jnp.where(((y_here + 4 - k) & 3) == y, live[k], value)
    return value


def turn_kernel(q0, q2, pair, out):
    x_here, y_here, _ = here()
    sub = lax.broadcasted_iota(jnp.int32, (128, 128), 0)
    lane = lax.broadcasted_iota(jnp.int32, (128, 128), 1)
    j = sub - 1
    source = (y_here + 4 - (j >> 3)) & 3
    pos = source * 32 + x_here * 8 + (j & 7)
    bar = jnp.where((sub >= 1) & (sub < 33) & (pos > lane), BIG, 0.0)
    aug = jnp.where(sub == 0, 1.0, bar).astype(BF)
    for k, q in enumerate((q0, pair.at[0:128], q2, pair.at[128:256])):
        for h in range(4):
            lanes = slice(h * 128, h * 128 + 128)
            out[k, 0:128, lanes] = q[:, lanes].astype(F32).T.astype(BF)
            out[k, 128:256, lanes] = aug


def turn(q, q2, pair):
    return pl.pallas_call(
        turn_kernel,
        in_specs=[VMEM] * 3,
        out_specs=VMEM,
        out_shape=jax.ShapeDtypeStruct((4, 256, 512), BF),
        compiler_params=pltpu.CompilerParams(vmem_limit_bytes=8 << 20),
        cost_estimate=cost(1),
        name="turn",
    )(q, q2, pair)


def attend(ks, spans, outs, qt, kk, vt, s_ref):
    units = [(i, t) for i in range(len(ks)) for t in range(len(spans) - 1)]

    def score(u):
        i, t = units[u]
        rows = slice(spans[t], spans[t + 1])
        size = spans[t + 1] - spans[t]
        s_ref[u % 2, 0:size] = jnp.dot(kk[rows], qt[ks[i]], preferred_element_type=F32)

    score(0)
    for u, (i, t) in enumerate(units):
        if u + 1 < len(units):
            score(u + 1)
        rows = slice(spans[t], spans[t + 1])
        s = s_ref[u % 2, 0 : spans[t + 1] - spans[t]]
        top = jnp.max(s, axis=0, keepdims=True)
        p = jnp.exp2((s - top) * LOG_SCALE)
        high = p.astype(BF)
        low = (p - high.astype(F32)).astype(BF)
        o = jnp.dot(vt[:, rows], high, preferred_element_type=F32)
        o += jnp.dot(vt[:, rows], low, preferred_element_type=F32)
        if t == 0:
            best, sums = top, o
        else:
            both = jnp.maximum(best, top)
            sums = sums * jnp.exp2((best - both) * LOG_SCALE) + o * jnp.exp2((top - both) * LOG_SCALE)
            best = both
        if t + 2 < len(spans):
            continue
        total = sums[128:129]
        mean = sums[0:128] / total
        most = jnp.maximum(jnp.max(jnp.abs(mean), axis=0, keepdims=True), 1e-30)
        den = jnp.log2(total) + best * LOG_SCALE
        num = den + jnp.log2(most)
        outs[i][0:128] = mean / most
        rows = []
        for x in (den, num):
            high = jnp.floor(x * 2.0 + 0.5) * 0.5
            rows += [high, x - high]
        outs[i][128:136] = jnp.concatenate(rows + [jnp.zeros((4, 512), F32)], axis=0)


def first_kernel(k, qt, mig, r0, r1, r2, r3, out, kk, vt, s_ref):
    fill(mig, (r0, r1, r2, r3), kk, vt)
    attend((k,), NARROW, (out,), qt, kk, vt, s_ref)


def more_kernel(ks, qt, kk, vt, *refs):
    attend(ks, WIDE, refs[-1 - len(ks) : -1], qt, kk, vt, refs[-1])


def cost(count):
    return pl.CostEstimate(
        flops=count << 20, transcendentals=count << 10, bytes_accessed=count << 16
    )


PART = jax.ShapeDtypeStruct((136, 512), F32)
def scores(spans):
    return pltpu.VMEM((2, max(b - a for a, b in zip(spans, spans[1:])), 512), F32)


def first(k, qt, mig, parts):
    return pl.pallas_call(
        functools.partial(first_kernel, k),
        in_specs=[VMEM] * 6,
        out_specs=[VMEM] * 3,
        out_shape=[
            PART,
            jax.ShapeDtypeStruct((ROWS, 256), BF),
            jax.ShapeDtypeStruct((144, ROWS), BF),
        ],
        scratch_shapes=[scores(NARROW)],
        compiler_params=pltpu.CompilerParams(vmem_limit_bytes=28 << 20),
        cost_estimate=cost(1),
        name="first",
    )(qt, mig, *parts)


def more(ks, qt, kk, vt, after=None):
    late = () if after is None else (after,)
    return pl.pallas_call(
        functools.partial(more_kernel, ks),
        in_specs=[VMEM] * 3 + [HBM] * len(late),
        out_specs=[VMEM] * len(ks),
        out_shape=[PART] * len(ks),
        scratch_shapes=[scores(WIDE)],
        compiler_params=pltpu.CompilerParams(vmem_limit_bytes=28 << 20),
        cost_estimate=cost(len(ks)),
        name="more",
    )(qt, kk, vt, *late)


def combine_kernel(g0, g2, g, out):
    parts = (g0, g2, g.at[0], g.at[1])
    dens = [x[128:129] + x[129:130] for x in parts]
    top = functools.reduce(jnp.maximum, dens)
    share = 1.0 / sum(jnp.exp2(x - top) for x in dens)
    result = sum(
        x[0:128] * (jnp.exp2(x[130:131] + x[131:132] - top) * share) for x in parts
    )
    for h in range(4):
        lanes = slice(h * 128, h * 128 + 128)
        out[:, lanes] = result[:, lanes].T.astype(BF)


def combine(*parts):
    return pl.pallas_call(
        combine_kernel,
        in_specs=[VMEM] * 3,
        out_specs=VMEM,
        out_shape=jax.ShapeDtypeStruct((128, 512), BF),
        compiler_params=pltpu.CompilerParams(vmem_limit_bytes=8 << 20),
        name="combine",
    )(*parts)


def shift(value, axis, k):
    return lax.ppermute(value, axis, [(i, (i + k) % 4) for i in range(4)])


def swap(value, k):
    return lax.ppermute(value, "x", [(i, i ^ k) for i in range(4)])


def local(queries, new_kv, pool, page_table, ctx_len, move_page, move_dest, append_page):
    fresh = new_kv[0]
    q = queries[0]
    mig = pack(page_table, move_page, move_dest, pool[0])
    after = mig
    mig = mig.reshape(INST * KVH, MOST * PAGE * 2, D)
    mig = lax.all_to_all(mig, ("ba", "y"), 0, 0, tiled=True)
    *parts, updated = settle(page_table, ctx_len, append_page, after, pool[0], fresh)
    parts = [r.reshape((REST + 4) * 2, D) for r in parts]
    parts = [parts[0]] + [shift(parts[k], "y", k) for k in range(1, 4)]
    q2 = swap(q, 2)
    far, updated = lax.optimization_barrier((q2, updated))
    pair = swap(jnp.concatenate([q, far], axis=0), 1)
    qt = turn(q, q2, pair)
    out2, kk, vt = first(2, qt, mig.reshape(MIG_ROWS // 128, 256, D), parts)
    got2 = swap(out2.astype(F16), 2).astype(F32)
    out1, out3 = more((1, 3), qt, kk, vt)
    sent = [swap(out.astype(F16), k) for k, out in ((1, out1), (3, out3))]
    got = jnp.stack(sent).astype(F32)
    (out0,) = more((0,), qt, kk, vt, after=got2)
    return combine(out0, got2, got)[None], updated[None]


def solution(mesh):
    grid = Mesh(np.asarray(mesh.devices).reshape(4, 4, 8), ("y", "x", "ba"))
    aa = ("y", "x")
    return jax.shard_map(
        local,
        mesh=grid,
        in_specs=(
            P("ba", None, aa),
            P("ba", aa, None, None),
            P("ba", aa, None, None, None),
            P("ba", aa),
            P("ba", aa),
            P("ba", aa),
            P("ba", aa),
            P("ba", aa),
        ),
        out_specs=(P("ba", None, aa), P("ba", aa, None, None, None)),
        check_vma=False,
    )
```

```python
import functools
import math

import jax
import jax.numpy as jnp
import numpy as np
from jax import lax
from jax.experimental import pallas as pl
from jax.experimental.pallas import tpu as pltpu
from jax.sharding import Mesh, PartitionSpec as P

D = 128
KVH = 4
MOST = 2
PAGE = 32
TABLE = 4
MOVES = 7
INST = 8
NEW_DEV = 8
NQ = 128
RES = TABLE * PAGE + NEW_DEV
DEAD = 128.0
BIG = -1e30
BF = jnp.bfloat16
F32 = jnp.float32
F16 = jnp.float16
LOG_SCALE = math.log2(math.e) / math.sqrt(D)
HALF = MOST * PAGE
REST = RES - HALF
MIG_ROWS = INST * KVH * MOST * PAGE
OLD_ROWS = (TABLE - MOST) * PAGE * KVH
ROWS = MIG_ROWS + OLD_ROWS + 128
SPANS = (0, 1280, ROWS)
SAMPLE = slice(MIG_ROWS - 128, MIG_ROWS)

SMEM = pl.BlockSpec(memory_space=pltpu.SMEM)
HBM = pl.BlockSpec(memory_space=pltpu.HBM)
VMEM = pl.BlockSpec(memory_space=pltpu.VMEM)


def here():
    return (
        lax.axis_index("x").astype(jnp.int32),
        lax.axis_index("y").astype(jnp.int32),
        lax.axis_index("ba").astype(jnp.int32),
    )


def pack_kernel(
    table_in, page_in, dest_in, source, mig, table, page, dest, pool, dead, sem_s, sem_p, sem_m
):
    third = source.shape[0] // 3
    fetch = [
        pltpu.make_async_copy(
            source.at[pl.ds(i * third, third)], pool.at[pl.ds(i * third, third)], sem_p.at[i]
        )
        for i in range(3)
    ]
    for copy in fetch:
        copy.start()
    scalars = [
        pltpu.make_async_copy(a, b, sem_s.at[i])
        for i, (a, b) in enumerate(((table_in, table), (page_in, page), (dest_in, dest)))
    ]
    for copy in scalars:
        copy.start()
    dead[...] = jnp.full_like(dead, DEAD)
    b_here = here()[2]
    for copy in scalars:
        copy.wait()
    for d in range(INST):
        count = jnp.int32(0)
        for m in range(MOVES):
            count += (dest[0, m] == d).astype(jnp.int32)
        for s in range(MOST):

            @pl.when((count <= s) & (b_here != d))
            def _():
                pltpu.make_async_copy(dead, mig.at[d, :, s], sem_m).start()

    for copy in fetch:
        copy.wait()
    for m in range(MOVES):
        rank = jnp.int32(0)
        for e in range(m):
            rank += (dest[0, e] == dest[0, m]).astype(jnp.int32)
        for y in range(KVH):
            pltpu.make_async_copy(
                pool.at[page[0, m], :, :, pl.ds(y * D, D)], mig.at[dest[0, m], y, rank], sem_m
            ).start()
    for j in range(MOST):
        for y in range(KVH):
            pltpu.make_async_copy(
                pool.at[table[0, j], :, :, pl.ds(y * D, D)], mig.at[b_here, y, j], sem_m
            ).start()
    pltpu.make_async_copy(mig, mig, sem_m).wait()


def pack(table, page, dest, pool):
    return pl.pallas_call(
        pack_kernel,
        in_specs=[HBM] * 4,
        out_specs=HBM,
        out_shape=jax.ShapeDtypeStruct((INST, KVH, MOST, PAGE, 2, D), BF),
        scratch_shapes=[pltpu.SMEM(a.shape, jnp.int32) for a in (table, page, dest)]
        + [
            pltpu.VMEM(pool.shape, BF),
            pltpu.VMEM((KVH, PAGE, 2, D), BF),
            pltpu.SemaphoreType.DMA((3,)),
            pltpu.SemaphoreType.DMA((3,)),
            pltpu.SemaphoreType.DMA,
        ],
        compiler_params=pltpu.CompilerParams(vmem_limit_bytes=60 << 20),
        name="pack",
    )(table, page, dest, pool)


def settle_kernel(
    table, ctx, page, after, source, new, r0, r1, r2, r3, target, pool, sem, sem_r
):
    fetch = pltpu.make_async_copy(source, pool, sem.at[0])
    fetch.start()
    y_here = here()[1]
    length = ctx[0, 0].astype(F32)
    fetch.wait()
    outs = (r0, r1, r2, r3)
    for k in range(4):
        lanes = pl.ds(pl.multiple_of(lax.rem(y_here + k, 4) * D, D), D)
        for j in range(MOST, TABLE):
            pltpu.make_async_copy(
                pool.at[table[0, j], :, :, lanes],
                outs[k].at[pl.ds((j - MOST) * PAGE, PAGE)],
                sem_r.at[k],
            ).start()
        outs[k][REST : REST + 4] = jnp.full((4, 2, D), length, F32).astype(BF)
        pltpu.make_async_copy(
            new.at[:, :, lanes], outs[k].at[pl.ds((TABLE - MOST) * PAGE, NEW_DEV)], sem_r.at[k]
        ).start()
    for k in range(4):
        moved = outs[k].at[pl.ds(0, REST)]
        pltpu.make_async_copy(moved, moved, sem_r.at[k]).wait()
    last = pltpu.make_async_copy(new, pool.at[page[0, 0], pl.ds(0, NEW_DEV)], sem.at[0])
    last.start()
    last.wait()
    copy = pltpu.make_async_copy(pool, target, sem.at[0])
    copy.start()
    copy.wait()


def settle(table, ctx, page, after, pool, new):
    return pl.pallas_call(
        settle_kernel,
        in_specs=[SMEM] * 3 + [HBM, HBM, VMEM],
        out_specs=[VMEM] * 4 + [HBM],
        out_shape=[jax.ShapeDtypeStruct((REST + 4, 2, D), BF)] * 4
        + [jax.ShapeDtypeStruct(pool.shape, BF)],
        scratch_shapes=[
            pltpu.VMEM(pool.shape, BF),
            pltpu.SemaphoreType.DMA((1,)),
            pltpu.SemaphoreType.DMA((4,)),
        ],
        compiler_params=pltpu.CompilerParams(vmem_limit_bytes=8 << 20),
        cost_estimate=cost(1),
        name="settle",
    )(table, ctx, page, after, pool, new)


def put(x, pick, kk, vt, at, marks=None):
    lane = lax.broadcasted_iota(jnp.int32, (128, 128), 1)
    keys = jnp.dot(pick[0], x, preferred_element_type=F32)
    kk[at, 0:128] = keys.astype(BF)
    if marks is None:
        marks = jnp.where((lane == 0) & (keys > 64.0), BIG, 0.0)
    kk[at, 128:256] = marks.astype(BF)
    vals = lax.dot_general(x, pick[1], (((0,), (0,)), ((), ())), preferred_element_type=F32)
    vt[0:128, at] = vals.astype(BF)


def fill(mig, parts, kk, vt):
    row = lax.broadcasted_iota(jnp.int32, (128, 256), 0)
    col = lax.broadcasted_iota(jnp.int32, (128, 256), 1)
    keys = (col == 2 * row).astype(BF)
    row = lax.broadcasted_iota(jnp.int32, (256, 128), 0)
    col = lax.broadcasted_iota(jnp.int32, (256, 128), 1)
    pick = (keys, (row == 2 * col + 1).astype(BF))
    vt[128:144, :] = jnp.ones((16, ROWS), BF)
    sub = lax.broadcasted_iota(jnp.int32, (128, 128), 0)
    lane = lax.broadcasted_iota(jnp.int32, (128, 128), 1)
    b_here = here()[2]
    live = [r[144:152].astype(F32)[0:1] for r in parts]
    row = sub.astype(F32)
    for i in range(MIG_ROWS // 128):
        source = lax.rem(b_here + 1 + (i >> 1), INST)
        x = mig[2 * source + (i & 1)]
        marks = None
        if i >= MIG_ROWS // 128 - 2:
            ctx = [live_of(live, 2 * (i & 1) + e) for e in range(2)]
            dead = row >= jnp.where(sub < 64, ctx[0], ctx[1] + 64.0)
            marks = jnp.where((lane == 0) & dead, BIG, 0.0)
        put(x, pick, kk, vt, slice(i * 128, i * 128 + 128), marks)
    for i in range(2):
        x = jnp.concatenate([parts[2 * i][0:128], parts[2 * i + 1][0:128]], axis=0)
        at = MIG_ROWS + i * 128
        dead = row >= jnp.where(sub < 64, live[2 * i] - 64.0, live[2 * i + 1])
        marks = jnp.where((lane == 0) & dead, BIG, 0.0)
        put(x, pick, kk, vt, slice(at, at + 128), marks)
    at = MIG_ROWS + OLD_ROWS
    x = jnp.concatenate([r[128:144] for r in parts] + [jnp.zeros((192, 128), BF)], axis=0)
    hot = jnp.where((lane == 1 + sub) & (sub < 32), 1.0, 0.0)
    marks = jnp.where((lane == 0) & (sub >= 32), BIG, hot)
    put(x, pick, kk, vt, slice(at, at + 128), marks)


def live_of(live, y):
    y_here = here()[1]
    value = live[0]
    for k in range(1, 4):
        value = jnp.where(((y_here + 4 - k) & 3) == y, live[k], value)
    return value


def turn_kernel(q0, q2, pair, out):
    x_here, y_here, _ = here()
    sub = lax.broadcasted_iota(jnp.int32, (128, 128), 0)
    lane = lax.broadcasted_iota(jnp.int32, (128, 128), 1)
    j = sub - 1
    source = (y_here + 4 - (j >> 3)) & 3
    pos = source * 32 + x_here * 8 + (j & 7)
    bar = jnp.where((sub >= 1) & (sub < 33) & (pos > lane), BIG, 0.0)
    aug = jnp.where(sub == 0, 1.0, bar).astype(BF)
    for k, q in enumerate((q0, pair.at[0:128], q2, pair.at[128:256])):
        for h in range(4):
            lanes = slice(h * 128, h * 128 + 128)
            out[k, 0:128, lanes] = q[:, lanes].astype(F32).T.astype(BF)
            out[k, 128:256, lanes] = aug


def turn(q, q2, pair):
    return pl.pallas_call(
        turn_kernel,
        in_specs=[VMEM] * 3,
        out_specs=VMEM,
        out_shape=jax.ShapeDtypeStruct((4, 256, 512), BF),
        compiler_params=pltpu.CompilerParams(vmem_limit_bytes=8 << 20),
        cost_estimate=cost(1),
        name="turn",
    )(q, q2, pair)


def emit(out, sums, top):
    total = sums[128:129]
    mean = sums[0:128] / total
    most = jnp.maximum(jnp.max(jnp.abs(mean), axis=0, keepdims=True), 1e-30)
    den = jnp.log2(total) + top * LOG_SCALE
    num = den + jnp.log2(most)
    out[0:128] = mean / most
    rows = []
    for x in (den, num):
        high = jnp.floor(x * 2.0 + 0.5) * 0.5
        rows += [high, x - high]
    out[128:136] = jnp.concatenate(rows + [jnp.zeros((4, 512), F32)], axis=0)


def weigh(s, top, values):
    p = jnp.exp2((s - top) * LOG_SCALE)
    high = p.astype(BF)
    low = (p - high.astype(F32)).astype(BF)
    o = jnp.dot(values, high, preferred_element_type=F32)
    return o + jnp.dot(values, low, preferred_element_type=F32)


def exact(q, out, kk, vt, s_ref):
    best = sums = None
    for start, stop in zip(SPANS, SPANS[1:]):
        rows = slice(start, stop)
        s_ref[0 : stop - start] = jnp.dot(kk[rows], q, preferred_element_type=F32)
        s = s_ref[0 : stop - start]
        top = jnp.max(s, axis=0, keepdims=True)
        o = weigh(s, top, vt[:, rows])
        if best is None:
            best, sums = top, o
        else:
            both = jnp.maximum(best, top)
            old = jnp.exp2((best - both) * LOG_SCALE)
            sums = sums * old + o * jnp.exp2((top - both) * LOG_SCALE)
            best = both
    emit(out, sums, best)


def attend(ks, outs, qt, kk, vt, s_ref):
    bad = []
    for k, out in zip(ks, outs):
        q = qt[k]
        top = jnp.max(jnp.dot(kk[SAMPLE], q, preferred_element_type=F32), axis=0, keepdims=True)
        sums = weigh(jnp.dot(kk[...], q, preferred_element_type=F32), top, vt[...])
        emit(out, sums, top)
        bad.append(jnp.max(jnp.where(sums[128:129] < 1e36, 0.0, 1.0)) > 0.5)
    for k, out, wrong in zip(ks, outs, bad):

        @pl.when(wrong)
        def _():
            exact(qt[k], out, kk, vt, s_ref)


def first_kernel(k, qt, mig, r0, r1, r2, r3, out, kk, vt, s_ref):
    fill(mig, (r0, r1, r2, r3), kk, vt)
    attend((k,), (out,), qt, kk, vt, s_ref)


def more_kernel(ks, qt, kk, vt, *refs):
    attend(ks, refs[-1 - len(ks) : -1], qt, kk, vt, refs[-1])


def cost(count):
    return pl.CostEstimate(
        flops=count << 20, transcendentals=count << 10, bytes_accessed=count << 16
    )


PART = jax.ShapeDtypeStruct((136, 512), F32)
SCORES = pltpu.VMEM((max(b - a for a, b in zip(SPANS, SPANS[1:])), 512), F32)


def first(k, qt, mig, parts):
    return pl.pallas_call(
        functools.partial(first_kernel, k),
        in_specs=[VMEM] * 6,
        out_specs=[VMEM] * 3,
        out_shape=[
            PART,
            jax.ShapeDtypeStruct((ROWS, 256), BF),
            jax.ShapeDtypeStruct((144, ROWS), BF),
        ],
        scratch_shapes=[SCORES],
        compiler_params=pltpu.CompilerParams(vmem_limit_bytes=28 << 20),
        cost_estimate=cost(1),
        name="first",
    )(qt, mig, *parts)


def more(ks, qt, kk, vt, after=None):
    late = () if after is None else (after,)
    return pl.pallas_call(
        functools.partial(more_kernel, ks),
        in_specs=[VMEM] * 3 + [HBM] * len(late),
        out_specs=[VMEM] * len(ks),
        out_shape=[PART] * len(ks),
        scratch_shapes=[SCORES],
        compiler_params=pltpu.CompilerParams(vmem_limit_bytes=28 << 20),
        cost_estimate=cost(len(ks)),
        name="more",
    )(qt, kk, vt, *late)


def combine_kernel(g0, g2, g, out):
    parts = (g0, g2, g.at[0], g.at[1])
    dens = [x[128:129] + x[129:130] for x in parts]
    top = functools.reduce(jnp.maximum, dens)
    share = 1.0 / sum(jnp.exp2(x - top) for x in dens)
    result = sum(
        x[0:128] * (jnp.exp2(x[130:131] + x[131:132] - top) * share) for x in parts
    )
    for h in range(4):
        lanes = slice(h * 128, h * 128 + 128)
        out[:, lanes] = result[:, lanes].T.astype(BF)


def combine(*parts):
    return pl.pallas_call(
        combine_kernel,
        in_specs=[VMEM] * 3,
        out_specs=VMEM,
        out_shape=jax.ShapeDtypeStruct((128, 512), BF),
        compiler_params=pltpu.CompilerParams(vmem_limit_bytes=8 << 20),
        name="combine",
    )(*parts)


def shift(value, axis, k):
    return lax.ppermute(value, axis, [(i, (i + k) % 4) for i in range(4)])


def swap(value, k):
    return lax.ppermute(value, "x", [(i, i ^ k) for i in range(4)])


def local(queries, new_kv, pool, page_table, ctx_len, move_page, move_dest, append_page):
    fresh = new_kv[0]
    q = queries[0]
    mig = pack(page_table, move_page, move_dest, pool[0])
    after = mig
    mig = mig.reshape(INST * KVH, MOST * PAGE * 2, D)
    mig = lax.all_to_all(mig, ("ba", "y"), 0, 0, tiled=True)
    *parts, updated = settle(page_table, ctx_len, append_page, after, pool[0], fresh)
    parts = [r.reshape((REST + 4) * 2, D) for r in parts]
    far = shift(parts[2], "y", 2)
    parts = [parts[0], shift(parts[1], "y", 1), far, shift(parts[3], "y", 3)]
    q2 = swap(q, 2)
    q2, updated = lax.optimization_barrier((q2, updated))
    pair = swap(jnp.concatenate([q, q2], axis=0), 1)
    qt = turn(q, q2, pair)
    out2, kk, vt = first(2, qt, mig.reshape(MIG_ROWS // 128, 256, D), parts)
    got2 = swap(out2.astype(F16), 2).astype(F32)
    out1, out3 = more((1, 3), qt, kk, vt)
    sent = [swap(out.astype(F16), k) for k, out in ((1, out1), (3, out3))]
    got = jnp.stack(sent).astype(F32)
    (out0,) = more((0,), qt, kk, vt, after=got2)
    return combine(out0, got2, got)[None], updated[None]


def solution(mesh):
    grid = Mesh(np.asarray(mesh.devices).reshape(4, 4, 8), ("y", "x", "ba"))
    aa = ("y", "x")
    return jax.shard_map(
        local,
        mesh=grid,
        in_specs=(
            P("ba", None, aa),
            P("ba", aa, None, None),
            P("ba", aa, None, None, None),
            P("ba", aa),
            P("ba", aa),
            P("ba", aa),
            P("ba", aa),
            P("ba", aa),
        ),
        out_specs=(P("ba", None, aa), P("ba", aa, None, None, None)),
        check_vma=False,
    )
```

```python
import functools
import math

import jax
import jax.numpy as jnp
import numpy as np
from jax import lax
from jax.experimental import pallas as pl
from jax.experimental.pallas import tpu as pltpu
from jax.sharding import Mesh, PartitionSpec as P

D = 128
KVH = 4
MOST = 2
PAGE = 32
TABLE = 4
MOVES = 7
INST = 8
NEW_DEV = 8
NQ = 128
RES = TABLE * PAGE + NEW_DEV
DEAD = 128.0
BIG = -1e30
BF = jnp.bfloat16
F32 = jnp.float32
F16 = jnp.float16
LOG_SCALE = math.log2(math.e) / math.sqrt(D)
HALF = MOST * PAGE
REST = RES - HALF
MIG_ROWS = INST * KVH * MOST * PAGE
OLD_ROWS = (TABLE - MOST) * PAGE * KVH
ROWS = MIG_ROWS + OLD_ROWS + 128
SPANS = (0, 1280, ROWS)
SAMPLE = slice(MIG_ROWS - 128, MIG_ROWS)

SMEM = pl.BlockSpec(memory_space=pltpu.SMEM)
HBM = pl.BlockSpec(memory_space=pltpu.HBM)
VMEM = pl.BlockSpec(memory_space=pltpu.VMEM)


def here():
    return (
        lax.axis_index("x").astype(jnp.int32),
        lax.axis_index("y").astype(jnp.int32),
        lax.axis_index("ba").astype(jnp.int32),
    )


def pack_kernel(
    table_in, page_in, dest_in, source, mig, table, page, dest, pool, dead, sem_s, sem_p, sem_m
):
    third = source.shape[0] // 3
    fetch = [
        pltpu.make_async_copy(
            source.at[pl.ds(i * third, third)], pool.at[pl.ds(i * third, third)], sem_p.at[i]
        )
        for i in range(3)
    ]
    for copy in fetch:
        copy.start()
    scalars = [
        pltpu.make_async_copy(a, b, sem_s.at[i])
        for i, (a, b) in enumerate(((table_in, table), (page_in, page), (dest_in, dest)))
    ]
    for copy in scalars:
        copy.start()
    dead[...] = jnp.full_like(dead, DEAD)
    b_here = here()[2]
    for copy in scalars:
        copy.wait()
    for d in range(INST):
        count = jnp.int32(0)
        for m in range(MOVES):
            count += (dest[0, m] == d).astype(jnp.int32)
        for s in range(MOST):

            @pl.when((count <= s) & (b_here != d))
            def _():
                pltpu.make_async_copy(dead, mig.at[d, :, s], sem_m).start()

    for copy in fetch:
        copy.wait()
    for m in range(MOVES):
        rank = jnp.int32(0)
        for e in range(m):
            rank += (dest[0, e] == dest[0, m]).astype(jnp.int32)
        for y in range(KVH):
            pltpu.make_async_copy(
                pool.at[page[0, m], :, :, pl.ds(y * D, D)], mig.at[dest[0, m], y, rank], sem_m
            ).start()
    for j in range(MOST):
        for y in range(KVH):
            pltpu.make_async_copy(
                pool.at[table[0, j], :, :, pl.ds(y * D, D)], mig.at[b_here, y, j], sem_m
            ).start()
    pltpu.make_async_copy(mig, mig, sem_m).wait()


def pack(table, page, dest, pool):
    return pl.pallas_call(
        pack_kernel,
        in_specs=[HBM] * 4,
        out_specs=HBM,
        out_shape=jax.ShapeDtypeStruct((INST, KVH, MOST, PAGE, 2, D), BF),
        scratch_shapes=[pltpu.SMEM(a.shape, jnp.int32) for a in (table, page, dest)]
        + [
            pltpu.VMEM(pool.shape, BF),
            pltpu.VMEM((KVH, PAGE, 2, D), BF),
            pltpu.SemaphoreType.DMA((3,)),
            pltpu.SemaphoreType.DMA((3,)),
            pltpu.SemaphoreType.DMA,
        ],
        compiler_params=pltpu.CompilerParams(vmem_limit_bytes=60 << 20),
        name="pack",
    )(table, page, dest, pool)


def settle_kernel(
    table, ctx, page, after, source, new, r0, r1, r2, r3, target, pool, sem, sem_r
):
    fetch = pltpu.make_async_copy(source, pool, sem.at[0])
    fetch.start()
    y_here = here()[1]
    length = ctx[0, 0].astype(F32)
    fetch.wait()
    outs = (r0, r1, r2, r3)
    for k in range(4):
        lanes = pl.ds(pl.multiple_of(lax.rem(y_here + k, 4) * D, D), D)
        for j in range(MOST, TABLE):
            pltpu.make_async_copy(
                pool.at[table[0, j], :, :, lanes],
                outs[k].at[pl.ds((j - MOST) * PAGE, PAGE)],
                sem_r.at[k],
            ).start()
        outs[k][REST : REST + 4] = jnp.full((4, 2, D), length, F32).astype(BF)
        pltpu.make_async_copy(
            new.at[:, :, lanes], outs[k].at[pl.ds((TABLE - MOST) * PAGE, NEW_DEV)], sem_r.at[k]
        ).start()
    for k in range(4):
        moved = outs[k].at[pl.ds(0, REST)]
        pltpu.make_async_copy(moved, moved, sem_r.at[k]).wait()
    last = pltpu.make_async_copy(new, pool.at[page[0, 0], pl.ds(0, NEW_DEV)], sem.at[0])
    last.start()
    last.wait()
    copy = pltpu.make_async_copy(pool, target, sem.at[0])
    copy.start()
    copy.wait()


def settle(table, ctx, page, after, pool, new):
    return pl.pallas_call(
        settle_kernel,
        in_specs=[SMEM] * 3 + [HBM, HBM, VMEM],
        out_specs=[VMEM] * 4 + [HBM],
        out_shape=[jax.ShapeDtypeStruct((REST + 4, 2, D), BF)] * 4
        + [jax.ShapeDtypeStruct(pool.shape, BF)],
        scratch_shapes=[
            pltpu.VMEM(pool.shape, BF),
            pltpu.SemaphoreType.DMA((1,)),
            pltpu.SemaphoreType.DMA((4,)),
        ],
        compiler_params=pltpu.CompilerParams(vmem_limit_bytes=8 << 20),
        cost_estimate=cost(1),
        name="settle",
    )(table, ctx, page, after, pool, new)


def put(x, pick, kk, vt, at, marks=None):
    lane = lax.broadcasted_iota(jnp.int32, (128, 128), 1)
    keys = jnp.dot(pick[0], x, preferred_element_type=F32)
    kk[at, 0:128] = keys.astype(BF)
    if marks is None:
        marks = jnp.where((lane == 0) & (keys > 64.0), BIG, 0.0)
    kk[at, 128:256] = marks.astype(BF)
    vals = lax.dot_general(x, pick[1], (((0,), (0,)), ((), ())), preferred_element_type=F32)
    vt[0:128, at] = vals.astype(BF)


def fill(mig, parts, kk, vt):
    row = lax.broadcasted_iota(jnp.int32, (128, 256), 0)
    col = lax.broadcasted_iota(jnp.int32, (128, 256), 1)
    keys = (col == 2 * row).astype(BF)
    row = lax.broadcasted_iota(jnp.int32, (256, 128), 0)
    col = lax.broadcasted_iota(jnp.int32, (256, 128), 1)
    pick = (keys, (row == 2 * col + 1).astype(BF))
    vt[128:144, :] = jnp.ones((16, ROWS), BF)
    sub = lax.broadcasted_iota(jnp.int32, (128, 128), 0)
    lane = lax.broadcasted_iota(jnp.int32, (128, 128), 1)
    b_here = here()[2]
    live = [r[144:152].astype(F32)[0:1] for r in parts]
    row = sub.astype(F32)
    for i in range(MIG_ROWS // 128):
        source = lax.rem(b_here + 1 + (i >> 1), INST)
        x = mig[2 * source + (i & 1)]
        marks = None
        if i >= MIG_ROWS // 128 - 2:
            ctx = [live_of(live, 2 * (i & 1) + e) for e in range(2)]
            dead = row >= jnp.where(sub < 64, ctx[0], ctx[1] + 64.0)
            marks = jnp.where((lane == 0) & dead, BIG, 0.0)
        put(x, pick, kk, vt, slice(i * 128, i * 128 + 128), marks)
    for i in range(2):
        x = jnp.concatenate([parts[2 * i][0:128], parts[2 * i + 1][0:128]], axis=0)
        at = MIG_ROWS + i * 128
        dead = row >= jnp.where(sub < 64, live[2 * i] - 64.0, live[2 * i + 1])
        marks = jnp.where((lane == 0) & dead, BIG, 0.0)
        put(x, pick, kk, vt, slice(at, at + 128), marks)
    at = MIG_ROWS + OLD_ROWS
    x = jnp.concatenate([r[128:144] for r in parts] + [jnp.zeros((192, 128), BF)], axis=0)
    hot = jnp.where((lane == 1 + sub) & (sub < 32), 1.0, 0.0)
    marks = jnp.where((lane == 0) & (sub >= 32), BIG, hot)
    put(x, pick, kk, vt, slice(at, at + 128), marks)


def live_of(live, y):
    y_here = here()[1]
    value = live[0]
    for k in range(1, 4):
        value = jnp.where(((y_here + 4 - k) & 3) == y, live[k], value)
    return value


def turn_kernel(q0, q2, pair, out):
    x_here, y_here, _ = here()
    sub = lax.broadcasted_iota(jnp.int32, (128, 128), 0)
    lane = lax.broadcasted_iota(jnp.int32, (128, 128), 1)
    j = sub - 1
    source = (y_here + 4 - (j >> 3)) & 3
    pos = source * 32 + x_here * 8 + (j & 7)
    bar = jnp.where((sub >= 1) & (sub < 33) & (pos > lane), BIG, 0.0)
    aug = jnp.where(sub == 0, 1.0, bar).astype(BF)
    for k, q in enumerate((q0, pair.at[0:128], q2, pair.at[128:256])):
        for h in range(4):
            lanes = slice(h * 128, h * 128 + 128)
            out[k, 0:128, lanes] = q[:, lanes].astype(F32).T.astype(BF)
            out[k, 128:256, lanes] = aug


def turn(q, q2, pair):
    return pl.pallas_call(
        turn_kernel,
        in_specs=[VMEM] * 3,
        out_specs=VMEM,
        out_shape=jax.ShapeDtypeStruct((4, 256, 512), BF),
        compiler_params=pltpu.CompilerParams(vmem_limit_bytes=8 << 20),
        cost_estimate=cost(1),
        name="turn",
    )(q, q2, pair)


def emit(out, sums, top):
    total = sums[128:129]
    mean = sums[0:128] / total
    most = jnp.maximum(jnp.max(jnp.abs(mean), axis=0, keepdims=True), 1e-30)
    den = jnp.log2(total) + top * LOG_SCALE
    num = den + jnp.log2(most)
    out[0:128] = mean / most
    rows = []
    for x in (den, num):
        high = jnp.floor(x * 2.0 + 0.5) * 0.5
        rows += [high, x - high]
    out[128:136] = jnp.concatenate(rows + [jnp.zeros((4, 512), F32)], axis=0)


def weigh(s, top, values):
    p = jnp.exp2((s - top) * LOG_SCALE)
    high = p.astype(BF)
    low = (p - high.astype(F32)).astype(BF)
    o = jnp.dot(values, high, preferred_element_type=F32)
    return o + jnp.dot(values, low, preferred_element_type=F32)


def exact(q, out, kk, vt, s_ref):
    best = sums = None
    for start, stop in zip(SPANS, SPANS[1:]):
        rows = slice(start, stop)
        s_ref[0 : stop - start] = jnp.dot(kk[rows], q, preferred_element_type=F32)
        s = s_ref[0 : stop - start]
        top = jnp.max(s, axis=0, keepdims=True)
        o = weigh(s, top, vt[:, rows])
        if best is None:
            best, sums = top, o
        else:
            both = jnp.maximum(best, top)
            old = jnp.exp2((best - both) * LOG_SCALE)
            sums = sums * old + o * jnp.exp2((top - both) * LOG_SCALE)
            best = both
    emit(out, sums, best)


def place_of(k):
    core = here()[2] & 1
    return {"near": 1 + 2 * core, "next": 3 - 2 * core}.get(k, k)


def attend(ks, outs, qt, kk, vt, s_ref):
    bad = []
    ks = [place_of(k) for k in ks]
    for k, out in zip(ks, outs):
        q = qt[k]
        top = jnp.max(jnp.dot(kk[SAMPLE], q, preferred_element_type=F32), axis=0, keepdims=True)
        sums = weigh(jnp.dot(kk[...], q, preferred_element_type=F32), top, vt[...])
        emit(out, sums, top)
        bad.append(jnp.max(jnp.where(sums[128:129] < 1e36, 0.0, 1.0)) > 0.5)
    for k, out, wrong in zip(ks, outs, bad):

        @pl.when(wrong)
        def _():
            exact(qt[k], out, kk, vt, s_ref)


def first_kernel(k, qt, mig, r0, r1, r2, r3, out, kk, vt, s_ref):
    fill(mig, (r0, r1, r2, r3), kk, vt)
    attend((k,), (out,), qt, kk, vt, s_ref)


def more_kernel(ks, qt, kk, vt, *refs):
    attend(ks, refs[-1 - len(ks) : -1], qt, kk, vt, refs[-1])


def cost(count):
    return pl.CostEstimate(
        flops=count << 20, transcendentals=count << 10, bytes_accessed=count << 16
    )


PART = jax.ShapeDtypeStruct((136, 512), F32)
SCORES = pltpu.VMEM((max(b - a for a, b in zip(SPANS, SPANS[1:])), 512), F32)


def first(k, qt, mig, parts):
    return pl.pallas_call(
        functools.partial(first_kernel, k),
        in_specs=[VMEM] * 6,
        out_specs=[VMEM] * 3,
        out_shape=[
            PART,
            jax.ShapeDtypeStruct((ROWS, 256), BF),
            jax.ShapeDtypeStruct((144, ROWS), BF),
        ],
        scratch_shapes=[SCORES],
        compiler_params=pltpu.CompilerParams(vmem_limit_bytes=28 << 20),
        cost_estimate=cost(1),
        name="first",
    )(qt, mig, *parts)


def more(ks, qt, kk, vt, late=()):
    return pl.pallas_call(
        functools.partial(more_kernel, ks),
        in_specs=[VMEM] * 3 + [HBM] * len(late),
        out_specs=[VMEM] * len(ks),
        out_shape=[PART] * len(ks),
        scratch_shapes=[SCORES],
        compiler_params=pltpu.CompilerParams(vmem_limit_bytes=28 << 20),
        cost_estimate=cost(len(ks)),
        name="more",
    )(qt, kk, vt, *late)


def combine_kernel(*refs):
    *parts, out = refs
    dens = [x[128:129] + x[129:130] for x in parts]
    top = functools.reduce(jnp.maximum, dens)
    share = 1.0 / sum(jnp.exp2(x - top) for x in dens)
    result = sum(
        x[0:128] * (jnp.exp2(x[130:131] + x[131:132] - top) * share) for x in parts
    )
    for h in range(4):
        lanes = slice(h * 128, h * 128 + 128)
        out[:, lanes] = result[:, lanes].T.astype(BF)


def combine(*parts):
    return pl.pallas_call(
        combine_kernel,
        in_specs=[VMEM] * 4,
        out_specs=VMEM,
        out_shape=jax.ShapeDtypeStruct((128, 512), BF),
        compiler_params=pltpu.CompilerParams(vmem_limit_bytes=8 << 20),
        name="combine",
    )(*parts)


def shift(value, axis, k):
    return lax.ppermute(value, axis, [(i, (i + k) % 4) for i in range(4)])


def swap(value, k):
    return lax.ppermute(value, "x", [(i, i ^ k) for i in range(4)])


def beside(value, turn):
    pairs = [(x * INST + b, (x ^ (1 + 2 * ((b + turn) % 2))) * INST + b) for x in range(4) for b in range(INST)]
    return lax.ppermute(value, ("x", "ba"), pairs)


def local(queries, new_kv, pool, page_table, ctx_len, move_page, move_dest, append_page):
    fresh = new_kv[0]
    q = queries[0]
    mig = pack(page_table, move_page, move_dest, pool[0])
    after = mig
    mig = mig.reshape(INST * KVH, MOST * PAGE * 2, D)
    mig = lax.all_to_all(mig, ("ba", "y"), 0, 0, tiled=True)
    *parts, updated = settle(page_table, ctx_len, append_page, after, pool[0], fresh)
    parts = [r.reshape((REST + 4) * 2, D) for r in parts]
    far = shift(parts[2], "y", 2)
    parts = [parts[0], shift(parts[1], "y", 1), far, shift(parts[3], "y", 3)]
    q2 = swap(q, 2)
    q2, updated = lax.optimization_barrier((q2, updated))
    pair = swap(jnp.concatenate([q, q2], axis=0), 1)
    qt = turn(q, q2, pair)
    out2, kk, vt = first(2, qt, mig.reshape(MIG_ROWS // 128, 256, D), parts)
    got2 = swap(out2.astype(F16), 2).astype(F32)
    (near,) = more(("near",), qt, kk, vt)
    got = beside(near.astype(F16), 0).astype(F32)
    (other,) = more(("next",), qt, kk, vt)
    last = beside(other.astype(F16), 1).astype(F32)
    (out0,) = more((0,), qt, kk, vt, late=(got2, got))
    return combine(out0, got2, got, last)[None], updated[None]


def solution(mesh):
    grid = Mesh(np.asarray(mesh.devices).reshape(4, 4, 8), ("y", "x", "ba"))
    aa = ("y", "x")
    return jax.shard_map(
        local,
        mesh=grid,
        in_specs=(
            P("ba", None, aa),
            P("ba", aa, None, None),
            P("ba", aa, None, None, None),
            P("ba", aa),
            P("ba", aa),
            P("ba", aa),
            P("ba", aa),
            P("ba", aa),
        ),
        out_specs=(P("ba", None, aa), P("ba", aa, None, None, None)),
        check_vma=False,
    )
```

```python
import functools
import math

import jax
import jax.numpy as jnp
import numpy as np
from jax import lax
from jax.experimental import pallas as pl
from jax.experimental.pallas import tpu as pltpu
from jax.sharding import Mesh, PartitionSpec as P

D = 128
KVH = 4
MOST = 2
PAGE = 32
TABLE = 4
MOVES = 7
INST = 8
NEW_DEV = 8
NQ = 128
RES = TABLE * PAGE + NEW_DEV
DEAD = 128.0
BIG = -1e30
BF = jnp.bfloat16
F32 = jnp.float32
F16 = jnp.float16
LOG_SCALE = math.log2(math.e) / math.sqrt(D)
HALF = MOST * PAGE
REST = RES - HALF
MIG_ROWS = INST * KVH * MOST * PAGE
OLD_ROWS = (TABLE - MOST) * PAGE * KVH
ROWS = MIG_ROWS + OLD_ROWS + KVH * NEW_DEV
SPANS = (0, 1280, ROWS)
SAMPLE = slice(MIG_ROWS - 128, MIG_ROWS)

SMEM = pl.BlockSpec(memory_space=pltpu.SMEM)
HBM = pl.BlockSpec(memory_space=pltpu.HBM)
VMEM = pl.BlockSpec(memory_space=pltpu.VMEM)


def here():
    return (
        lax.axis_index("x").astype(jnp.int32),
        lax.axis_index("y").astype(jnp.int32),
        lax.axis_index("ba").astype(jnp.int32),
    )


def pack_kernel(
    table_in, page_in, dest_in, source, mig, table, page, dest, pool, dead, sem_s, sem_p, sem_m
):
    third = source.shape[0] // 3
    fetch = [
        pltpu.make_async_copy(
            source.at[pl.ds(i * third, third)], pool.at[pl.ds(i * third, third)], sem_p.at[i]
        )
        for i in range(3)
    ]
    for copy in fetch:
        copy.start()
    scalars = [
        pltpu.make_async_copy(a, b, sem_s.at[i])
        for i, (a, b) in enumerate(((table_in, table), (page_in, page), (dest_in, dest)))
    ]
    for copy in scalars:
        copy.start()
    dead[...] = jnp.full_like(dead, DEAD)
    b_here = here()[2]
    for copy in scalars:
        copy.wait()
    for d in range(INST):
        count = jnp.int32(0)
        for m in range(MOVES):
            count += (dest[0, m] == d).astype(jnp.int32)
        for s in range(MOST):

            @pl.when((count <= s) & (b_here != d))
            def _():
                pltpu.make_async_copy(dead, mig.at[d, :, s], sem_m).start()

    for copy in fetch:
        copy.wait()
    for m in range(MOVES):
        rank = jnp.int32(0)
        for e in range(m):
            rank += (dest[0, e] == dest[0, m]).astype(jnp.int32)
        for y in range(KVH):
            pltpu.make_async_copy(
                pool.at[page[0, m], :, :, pl.ds(y * D, D)], mig.at[dest[0, m], y, rank], sem_m
            ).start()
    for j in range(MOST):
        for y in range(KVH):
            pltpu.make_async_copy(
                pool.at[table[0, j], :, :, pl.ds(y * D, D)], mig.at[b_here, y, j], sem_m
            ).start()
    pltpu.make_async_copy(mig, mig, sem_m).wait()


def pack(table, page, dest, pool):
    return pl.pallas_call(
        pack_kernel,
        in_specs=[HBM] * 4,
        out_specs=HBM,
        out_shape=jax.ShapeDtypeStruct((INST, KVH, MOST, PAGE, 2, D), BF),
        scratch_shapes=[pltpu.SMEM(a.shape, jnp.int32) for a in (table, page, dest)]
        + [
            pltpu.VMEM(pool.shape, BF),
            pltpu.VMEM((KVH, PAGE, 2, D), BF),
            pltpu.SemaphoreType.DMA((3,)),
            pltpu.SemaphoreType.DMA((3,)),
            pltpu.SemaphoreType.DMA,
        ],
        compiler_params=pltpu.CompilerParams(vmem_limit_bytes=60 << 20),
        name="pack",
    )(table, page, dest, pool)


def settle_kernel(
    table, ctx, page, after, source, new, r0, r1, r2, r3, target, pool, sem, sem_r
):
    fetch = pltpu.make_async_copy(source, pool, sem.at[0])
    fetch.start()
    y_here = here()[1]
    length = ctx[0, 0].astype(F32)
    fetch.wait()
    outs = (r0, r1, r2, r3)
    for k in range(4):
        lanes = pl.ds(pl.multiple_of(lax.rem(y_here + k, 4) * D, D), D)
        for j in range(MOST, TABLE):
            pltpu.make_async_copy(
                pool.at[table[0, j], :, :, lanes],
                outs[k].at[pl.ds((j - MOST) * PAGE, PAGE)],
                sem_r.at[k],
            ).start()
        outs[k][REST : REST + 4] = jnp.full((4, 2, D), length, F32).astype(BF)
        pltpu.make_async_copy(
            new.at[:, :, lanes], outs[k].at[pl.ds((TABLE - MOST) * PAGE, NEW_DEV)], sem_r.at[k]
        ).start()
    for k in range(4):
        moved = outs[k].at[pl.ds(0, REST)]
        pltpu.make_async_copy(moved, moved, sem_r.at[k]).wait()
    last = pltpu.make_async_copy(new, pool.at[page[0, 0], pl.ds(0, NEW_DEV)], sem.at[0])
    last.start()
    last.wait()
    copy = pltpu.make_async_copy(pool, target, sem.at[0])
    copy.start()
    copy.wait()


def settle(table, ctx, page, after, pool, new):
    return pl.pallas_call(
        settle_kernel,
        in_specs=[SMEM] * 3 + [HBM, HBM, VMEM],
        out_specs=[VMEM] * 4 + [HBM],
        out_shape=[jax.ShapeDtypeStruct((REST + 4, 2, D), BF)] * 4
        + [jax.ShapeDtypeStruct(pool.shape, BF)],
        scratch_shapes=[
            pltpu.VMEM(pool.shape, BF),
            pltpu.SemaphoreType.DMA((1,)),
            pltpu.SemaphoreType.DMA((4,)),
        ],
        compiler_params=pltpu.CompilerParams(vmem_limit_bytes=8 << 20),
        cost_estimate=cost(1),
        name="settle",
    )(table, ctx, page, after, pool, new)


def put(x, pick, kk, vt, at, marks=None):
    lane = lax.broadcasted_iota(jnp.int32, (128, 128), 1)
    size = at.stop - at.start
    keys = jnp.dot(pick[0], x, preferred_element_type=F32)
    kk[at, 0:128] = keys[0:size].astype(BF)
    if marks is None:
        marks = jnp.where((lane == 0) & (keys > 64.0), BIG, 0.0)
    kk[at, 128:256] = marks[0:size].astype(BF)
    vals = lax.dot_general(x, pick[1], (((0,), (0,)), ((), ())), preferred_element_type=F32)
    vt[0:128, at] = vals[:, 0:size].astype(BF)


def fill(mig, parts, kk, vt):
    row = lax.broadcasted_iota(jnp.int32, (128, 256), 0)
    col = lax.broadcasted_iota(jnp.int32, (128, 256), 1)
    keys = (col == 2 * row).astype(BF)
    row = lax.broadcasted_iota(jnp.int32, (256, 128), 0)
    col = lax.broadcasted_iota(jnp.int32, (256, 128), 1)
    pick = (keys, (row == 2 * col + 1).astype(BF))
    vt[128:144, :] = jnp.ones((16, ROWS), BF)
    sub = lax.broadcasted_iota(jnp.int32, (128, 128), 0)
    lane = lax.broadcasted_iota(jnp.int32, (128, 128), 1)
    b_here = here()[2]
    live = [r[144:152].astype(F32)[0:1] for r in parts]
    row = sub.astype(F32)
    for i in range(MIG_ROWS // 128):
        source = lax.rem(b_here + 1 + (i >> 1), INST)
        x = mig[2 * source + (i & 1)]
        marks = None
        if i >= MIG_ROWS // 128 - 2:
            ctx = [live_of(live, 2 * (i & 1) + e) for e in range(2)]
            dead = row >= jnp.where(sub < 64, ctx[0], ctx[1] + 64.0)
            marks = jnp.where((lane == 0) & dead, BIG, 0.0)
        put(x, pick, kk, vt, slice(i * 128, i * 128 + 128), marks)
    for i in range(2):
        x = jnp.concatenate([parts[2 * i][0:128], parts[2 * i + 1][0:128]], axis=0)
        at = MIG_ROWS + i * 128
        dead = row >= jnp.where(sub < 64, live[2 * i] - 64.0, live[2 * i + 1])
        marks = jnp.where((lane == 0) & dead, BIG, 0.0)
        put(x, pick, kk, vt, slice(at, at + 128), marks)
    at = MIG_ROWS + OLD_ROWS
    x = jnp.concatenate([r[128:144] for r in parts] + [jnp.zeros((192, 128), BF)], axis=0)
    hot = jnp.where((lane == 1 + sub) & (sub < 32), 1.0, 0.0)
    marks = jnp.where((lane == 0) & (sub >= 32), BIG, hot)
    put(x, pick, kk, vt, slice(at, ROWS), marks)


def live_of(live, y):
    y_here = here()[1]
    value = live[0]
    for k in range(1, 4):
        value = jnp.where(((y_here + 4 - k) & 3) == y, live[k], value)
    return value


def turn_kernel(q0, q2, pair, out):
    x_here, y_here, _ = here()
    sub = lax.broadcasted_iota(jnp.int32, (128, 128), 0)
    lane = lax.broadcasted_iota(jnp.int32, (128, 128), 1)
    j = sub - 1
    source = (y_here + 4 - (j >> 3)) & 3
    pos = source * 32 + x_here * 8 + (j & 7)
    bar = jnp.where((sub >= 1) & (sub < 33) & (pos > lane), BIG, 0.0)
    aug = jnp.where(sub == 0, 1.0, bar).astype(BF)
    for k, q in enumerate((q0, pair.at[0:128], q2, pair.at[128:256])):
        for h in range(4):
            lanes = slice(h * 128, h * 128 + 128)
            out[k, 0:128, lanes] = q[:, lanes].astype(F32).T.astype(BF)
            out[k, 128:256, lanes] = aug


def turn(q, q2, pair):
    return pl.pallas_call(
        turn_kernel,
        in_specs=[VMEM] * 3,
        out_specs=VMEM,
        out_shape=jax.ShapeDtypeStruct((4, 256, 512), BF),
        compiler_params=pltpu.CompilerParams(vmem_limit_bytes=8 << 20),
        cost_estimate=cost(1),
        name="turn",
    )(q, q2, pair)


def emit(out, sums, top):
    total = sums[128:129]
    mean = sums[0:128] / total
    most = jnp.maximum(jnp.max(jnp.abs(mean), axis=0, keepdims=True), 1e-30)
    den = jnp.log2(total) + top * LOG_SCALE
    num = den + jnp.log2(most)
    out[0:128] = mean / most
    rows = []
    for x in (den, num):
        high = jnp.floor(x * 2.0 + 0.5) * 0.5
        rows += [high, x - high]
    out[128:136] = jnp.concatenate(rows + [jnp.zeros((4, 512), F32)], axis=0)


def weigh(s, top, values):
    p = jnp.exp2((s - top) * LOG_SCALE)
    high = p.astype(BF)
    low = (p - high.astype(F32)).astype(BF)
    o = jnp.dot(values, high, preferred_element_type=F32)
    return o + jnp.dot(values, low, preferred_element_type=F32)


def exact(q, out, kk, vt, s_ref):
    best = sums = None
    for start, stop in zip(SPANS, SPANS[1:]):
        rows = slice(start, stop)
        s_ref[0 : stop - start] = jnp.dot(kk[rows], q, preferred_element_type=F32)
        s = s_ref[0 : stop - start]
        top = jnp.max(s, axis=0, keepdims=True)
        o = weigh(s, top, vt[:, rows])
        if best is None:
            best, sums = top, o
        else:
            both = jnp.maximum(best, top)
            old = jnp.exp2((best - both) * LOG_SCALE)
            sums = sums * old + o * jnp.exp2((top - both) * LOG_SCALE)
            best = both
    emit(out, sums, best)


def attend(ks, outs, qt, kk, vt, s_ref):
    bad = []
    for k, out in zip(ks, outs):
        q = qt[k]
        top = jnp.max(jnp.dot(kk[SAMPLE], q, preferred_element_type=F32), axis=0, keepdims=True)
        sums = weigh(jnp.dot(kk[...], q, preferred_element_type=F32), top, vt[...])
        emit(out, sums, top)
        bad.append(jnp.max(jnp.where(sums[128:129] < 1e36, 0.0, 1.0)) > 0.5)
    for k, out, wrong in zip(ks, outs, bad):

        @pl.when(wrong)
        def _():
            exact(qt[k], out, kk, vt, s_ref)


def first_kernel(k, qt, mig, r0, r1, r2, r3, out, kk, vt, s_ref):
    fill(mig, (r0, r1, r2, r3), kk, vt)
    attend((k,), (out,), qt, kk, vt, s_ref)


def more_kernel(ks, qt, kk, vt, *refs):
    attend(ks, refs[-1 - len(ks) : -1], qt, kk, vt, refs[-1])


def cost(count):
    return pl.CostEstimate(
        flops=count << 20, transcendentals=count << 10, bytes_accessed=count << 16
    )


PART = jax.ShapeDtypeStruct((136, 512), F32)
SCORES = pltpu.VMEM((max(b - a for a, b in zip(SPANS, SPANS[1:])), 512), F32)


def first(k, qt, mig, parts):
    return pl.pallas_call(
        functools.partial(first_kernel, k),
        in_specs=[VMEM] * 6,
        out_specs=[VMEM] * 3,
        out_shape=[
            PART,
            jax.ShapeDtypeStruct((ROWS, 256), BF),
            jax.ShapeDtypeStruct((144, ROWS), BF),
        ],
        scratch_shapes=[SCORES],
        compiler_params=pltpu.CompilerParams(vmem_limit_bytes=28 << 20),
        cost_estimate=cost(1),
        name="first",
    )(qt, mig, *parts)


def more(ks, qt, kk, vt, after=None):
    late = () if after is None else (after,)
    return pl.pallas_call(
        functools.partial(more_kernel, ks),
        in_specs=[VMEM] * 3 + [HBM] * len(late),
        out_specs=[VMEM] * len(ks),
        out_shape=[PART] * len(ks),
        scratch_shapes=[SCORES],
        compiler_params=pltpu.CompilerParams(vmem_limit_bytes=28 << 20),
        cost_estimate=cost(len(ks)),
        name="more",
    )(qt, kk, vt, *late)


def combine_kernel(g0, g2, g, out):
    parts = (g0, g2, g.at[0], g.at[1])
    dens = [x[128:129] + x[129:130] for x in parts]
    top = functools.reduce(jnp.maximum, dens)
    share = 1.0 / sum(jnp.exp2(x - top) for x in dens)
    result = sum(
        x[0:128] * (jnp.exp2(x[130:131] + x[131:132] - top) * share) for x in parts
    )
    for h in range(4):
        lanes = slice(h * 128, h * 128 + 128)
        out[:, lanes] = result[:, lanes].T.astype(BF)


def combine(*parts):
    return pl.pallas_call(
        combine_kernel,
        in_specs=[VMEM] * 3,
        out_specs=VMEM,
        out_shape=jax.ShapeDtypeStruct((128, 512), BF),
        compiler_params=pltpu.CompilerParams(vmem_limit_bytes=8 << 20),
        name="combine",
    )(*parts)


def shift(value, axis, k):
    return lax.ppermute(value, axis, [(i, (i + k) % 4) for i in range(4)])


def swap(value, k):
    return lax.ppermute(value, "x", [(i, i ^ k) for i in range(4)])


def local(queries, new_kv, pool, page_table, ctx_len, move_page, move_dest, append_page):
    fresh = new_kv[0]
    q = queries[0]
    mig = pack(page_table, move_page, move_dest, pool[0])
    after = mig
    mig = mig.reshape(INST * KVH, MOST * PAGE * 2, D)
    mig = lax.all_to_all(mig, ("ba", "y"), 0, 0, tiled=True)
    *parts, updated = settle(page_table, ctx_len, append_page, after, pool[0], fresh)
    parts = [r.reshape((REST + 4) * 2, D) for r in parts]
    far = shift(parts[2], "y", 2)
    parts = [parts[0], shift(parts[1], "y", 1), far, shift(parts[3], "y", 3)]
    q2 = swap(q, 2)
    q2, updated = lax.optimization_barrier((q2, updated))
    pair = swap(jnp.concatenate([q, q2], axis=0), 1)
    qt = turn(q, q2, pair)
    out2, kk, vt = first(2, qt, mig.reshape(MIG_ROWS // 128, 256, D), parts)
    got2 = swap(out2.astype(F16), 2).astype(F32)
    out1, out3 = more((1, 3), qt, kk, vt)
    sent = [swap(out.astype(F16), k) for k, out in ((1, out1), (3, out3))]
    got = jnp.stack(sent).astype(F32)
    (out0,) = more((0,), qt, kk, vt, after=got2)
    return combine(out0, got2, got)[None], updated[None]


def solution(mesh):
    grid = Mesh(np.asarray(mesh.devices).reshape(4, 4, 8), ("y", "x", "ba"))
    aa = ("y", "x")
    return jax.shard_map(
        local,
        mesh=grid,
        in_specs=(
            P("ba", None, aa),
            P("ba", aa, None, None),
            P("ba", aa, None, None, None),
            P("ba", aa),
            P("ba", aa),
            P("ba", aa),
            P("ba", aa),
            P("ba", aa),
        ),
        out_specs=(P("ba", None, aa), P("ba", aa, None, None, None)),
        check_vma=False,
    )
```
